32 devices in a mesh: coil: 4 (over y, x), slab: 8 (over z, core).
Axes of the slice: x: 2, y: 2, z: 4, core: 2. Of those that a mesh axis runs over, the one named last changes fastest.
Arguments:
- warm_start: float32 [4, 2, 32, 128, 128], P('coil', None, 'slab'), may hold values from -6 to 6
- scaled_dual: float32 [4, 2, 32, 128, 128], P('coil', None, 'slab'), may hold values from -6 to 6
- consensus: float32 [2, 32, 128, 128], P(None, 'slab'), may hold values from -6 to 6
- kspace: float32 [4, 2, 32, 128, 128], P('coil', None, None, 'slab'), may hold values from -6 to 6
- coil_maps: float32 [4, 2, 32, 128, 128], P('coil', None, 'slab'), may hold values from -16 to 16
- line_mask: int32 [32, 128], replicated, may hold values 0 or 1
Outputs:
- new_consensus: float32 [2, 32, 128, 128], P(None, 'slab')
- new_dual: float32 [4, 2, 32, 128, 128], P('coil', None, 'slab')
The draws below stay inside these ranges and needn't reach their ends.
All inputs are finite; a program needn't handle non-finite values.
Results may differ from the reference program's by a relative error of at most 0.00007.
Values sent between devices are 32-bit elements; how exact they have to be, the bound alone decides.
No kernel may reach another device: no remote copies, remote signals or barrier semaphores. Data moves between devices by JAX's collectives and lax.ppermute only.
A program may use at most 64 MiB of HBM per device.

```python
import jax
import jax.numpy as jnp
from jax import lax

NX = 128
NY = 128
NZ = 32
COILS = 4


def draw_coil_maps(key, part):
    subkeys = jax.random.split(key, 3)
    shape = (COILS, 2, NZ, NX, NY)
    base_draw = jnp.clip(jax.random.normal(subkeys[0], shape, jnp.float32), -3.0, 3.0)
    spread = 0.6
    plane_scale = jax.random.uniform(subkeys[1], (COILS, 1, NZ, 1, 1), jnp.float32, -spread, spread)
    row_scale = jax.random.uniform(subkeys[2], (COILS, 1, 1, NX, 1), jnp.float32, -spread, spread)
    return base_draw * jnp.exp(plane_scale + row_scale)


def plant(drawn, own_key, least, largest):
    dims = drawn.shape
    spot = [jax.random.randint(jax.random.fold_in(own_key, axis), (), 0, dims[axis]) for axis in range(len(dims))]
    drawn = drawn.at[tuple(spot)].set(least)
    longest = dims.index(max(dims))
    spot[longest] = (spot[longest] + 1) % dims[longest]
    return drawn.at[tuple(spot)].set(largest)


def level_of(rng, extent, shards, least, high):
    loudness = 1.0
    for dim, shards_of in shards:
        draws = jax.random.uniform(jax.random.fold_in(jax.random.fold_in(rng, 6), dim), (shards_of,), jnp.float32, least / len(shards), high / len(shards))
        loudness = loudness * jnp.repeat(jnp.exp(draws), extent[dim] // shards_of).reshape((-1,) + (1,) * (len(extent) - 1 - dim))
    return loudness


def bell_draw(stream_key, dims, scale, reach, pieces=(), kind=jnp.bfloat16):
    gain = level_of(stream_key, dims, pieces, -0.22, 0.18) if pieces else 1.0
    array = jax.random.normal(stream_key, dims, jnp.float32) * scale * gain
    return jnp.minimum(jnp.maximum(array, -reach), reach).astype(kind)


def setup_inputs(seed: int = 0) -> dict:
    streams_of = jax.random.split(jax.random.key(seed), 7)
    warm_start = bell_draw(streams_of[0], (COILS, 2, NZ, NX, NY), 1.0, 6.0, ((0, 4), (2, 8)), jnp.float32)
    scaled_dual = bell_draw(streams_of[1], (COILS, 2, NZ, NX, NY), 1.0, 6.0, ((0, 4), (2, 8)), jnp.float32)
    consensus = bell_draw(streams_of[2], (2, NZ, NX, NY), 1.0, 6.0, ((1, 8),), jnp.float32)
    kspace = bell_draw(streams_of[3], (COILS, 2, NZ, NX, NY), 1.0, 6.0, ((0, 4), (3, 8)), jnp.float32)
    coil_maps = draw_coil_maps(jax.random.fold_in(streams_of[6], 71), 0)
    line_mask = plant((jax.random.randint(streams_of[5], (NZ, NY), 0, 8) < 1).astype(jnp.int32), jax.random.fold_in(streams_of[5], 1), 0, 1)
    return {"warm_start": warm_start, "scaled_dual": scaled_dual, "consensus": consensus, "kspace": kspace, "coil_maps": coil_maps, "line_mask": line_mask}


PENALTY = 1.0
THRESHOLD = 0.15
ROOT_HALF = 0.7071067811865476

def complex_of(pair):
    return pair[0] + 1j * pair[1]

def pair_of(values):
    return jnp.stack([jnp.real(values), jnp.imag(values)])

def haar_pairs(volume, dim_index):
    length = volume.shape[dim_index]
    even_cells = lax.slice_in_dim(volume, 0, length, 2, dim_index)
    odd_cells = lax.slice_in_dim(volume, 1, length, 2, dim_index)
    return jnp.concatenate([(even_cells + odd_cells) * ROOT_HALF, (even_cells - odd_cells) * ROOT_HALF], axis=dim_index)

def haar_unpairs(volume, dim_index):
    half_len = volume.shape[dim_index] // 2
    low_band = lax.slice_in_dim(volume, 0, half_len, 1, dim_index)
    high_band = lax.slice_in_dim(volume, half_len, 2 * half_len, 1, dim_index)
    even_cells = (low_band + high_band) * ROOT_HALF
    odd_cells = (low_band - high_band) * ROOT_HALF
    stacked = jnp.stack([even_cells, odd_cells], axis=dim_index + 1)
    return stacked.reshape(volume.shape)

def denoise(volume):
    coefficients = haar_pairs(haar_pairs(haar_pairs(volume, 1), 2), 3)
    depth, rows, width = (volume.shape[1], volume.shape[2], volume.shape[3])
    low_depth = jnp.arange(depth) < depth // 2
    low_rows = jnp.arange(rows) < rows // 2
    low_width = jnp.arange(width) < width // 2
    keep_mask = low_depth[:, None, None] & low_rows[None, :, None] & low_width[None, None, :]
    magnitude = jnp.sqrt(coefficients[0] * coefficients[0] + coefficients[1] * coefficients[1])
    factor = jnp.maximum(magnitude - THRESHOLD, 0.0) / jnp.maximum(magnitude, THRESHOLD)
    factor = jnp.where(keep_mask, jnp.ones_like(factor), factor)
    shrunk = coefficients * factor[None]
    return haar_unpairs(haar_unpairs(haar_unpairs(shrunk, 3), 2), 1)

def reference(warm_start, scaled_dual, consensus, kspace, coil_maps, line_mask):
    weight = line_mask.astype(warm_start.dtype)[:, None, :]
    target = complex_of(consensus)

    def solve_coil(items):
        start_pair, dual_pair, measured_pair, profile_pair = items
        profile = complex_of(profile_pair)
        measured = complex_of(measured_pair)

        def forward(volume):
            return weight * jnp.fft.fftn(profile * volume, axes=(0, 1, 2), norm='ortho')

        def adjoint(samples):
            return jnp.conj(profile) * jnp.fft.ifftn(weight * samples, axes=(0, 1, 2), norm='ortho')

        def normal_apply(volume):
            return adjoint(forward(volume)) + PENALTY * volume

        def inner_sum(first, second):
            return jnp.sum(jnp.real(jnp.conj(first) * second))
        start_field = complex_of(start_pair)
        dual_field = complex_of(dual_pair)
        residual = adjoint(measured - forward(start_field)) + PENALTY * (target - dual_field - start_field)
        norm_first = inner_sum(residual, residual)
        applied = normal_apply(residual)
        alpha_first = norm_first / inner_sum(residual, applied)
        iterate = start_field + alpha_first * residual
        residual_next = residual - alpha_first * applied
        norm_second = inner_sum(residual_next, residual_next)
        direction = residual_next + norm_second / norm_first * residual
        applied_next = normal_apply(direction)
        alpha_second = norm_second / inner_sum(direction, applied_next)
        solved = iterate + alpha_second * direction
        return pair_of(solved)
    solved_all = lax.map(solve_coil, (warm_start, scaled_dual, kspace, coil_maps))
    mixture = lax.optimization_barrier(jnp.mean(solved_all + scaled_dual, axis=0))
    new_consensus = denoise(mixture)
    new_dual = scaled_dual + solved_all - new_consensus[None]
    return (new_consensus, new_dual)
```

```python
import functools
import math

import jax
import jax.numpy as jnp
import numpy as np
from jax import lax
from jax.experimental import pallas as pl
from jax.experimental.pallas import tpu as pltpu
from jax.sharding import PartitionSpec as P

THRESHOLD = 0.15
ROOT_HALF = 0.7071067811865476
UNSEEN = 1e-20
F32 = jnp.float32
BF16 = jnp.bfloat16


def dft_table(length):
    index = np.arange(length)
    angles = (np.outer(index, index) % length) * (2.0 * math.pi / length)
    cosine = np.cos(angles) / math.sqrt(length)
    sine = np.sin(angles) / math.sqrt(length)
    whole = np.block([[cosine, sine], [-sine, cosine]]).astype(np.float32)
    high = whole.astype(jnp.bfloat16)
    low = (whole - high.astype(np.float32)).astype(jnp.bfloat16)
    return np.stack([high, low])


def halves(values):
    high = values.astype(BF16)
    return high, (values - high.astype(F32)).astype(BF16)


def contract(left, right, dims):
    return lax.dot_general(left, right, (dims, ((), ())), preferred_element_type=F32)


def rows_times_table(values, table_ref):
    high, low = halves(values)
    dims = ((1,), (1,))
    return (
        contract(high, table_ref[0], dims)
        + contract(high, table_ref[1], dims)
        + contract(low, table_ref[0], dims)
    )


def table_times_columns(table_ref, values):
    high, low = halves(values)
    dims = ((1,), (0,))
    return (
        contract(table_ref[0], high, dims)
        + contract(table_ref[1], high, dims)
        + contract(table_ref[0], low, dims)
    )


def fourier(real, imag, sign):
    count = len(real)
    if count == 1:
        return list(real), list(imag)
    if count % 2:
        out_real, out_imag = [], []
        for k in range(count):
            sum_real, sum_imag = real[0], imag[0]
            for n in range(1, count):
                angle = sign * 2.0 * math.pi * (k * n % count) / count
                c, s = math.cos(angle), math.sin(angle)
                sum_real = sum_real + (c * real[n] - s * imag[n])
                sum_imag = sum_imag + (c * imag[n] + s * real[n])
            out_real.append(sum_real)
            out_imag.append(sum_imag)
        return out_real, out_imag
    even_real, even_imag = fourier(real[0::2], imag[0::2], sign)
    odd_real, odd_imag = fourier(real[1::2], imag[1::2], sign)
    half = count // 2
    out_real, out_imag = [None] * count, [None] * count
    for k in range(half):
        x, y = odd_real[k], odd_imag[k]
        if k == 0:
            pass
        elif 4 * k == count:
            x, y = (-y, x) if sign > 0 else (y, -x)
        elif 8 * k == count:
            x, y = (x - sign * y) * ROOT_HALF, (y + sign * x) * ROOT_HALF
        elif 8 * k == 3 * count:
            x, y = (-x - sign * y) * ROOT_HALF, (sign * x - y) * ROOT_HALF
        else:
            angle = sign * 2.0 * math.pi * k / count
            c, s = math.cos(angle), math.sin(angle)
            x, y = c * x - s * y, c * y + s * x
        out_real[k], out_imag[k] = even_real[k] + x, even_imag[k] + y
        out_real[k + half], out_imag[k + half] = even_real[k] - x, even_imag[k] - y
    return out_real, out_imag


def total(values):
    return jnp.sum(values, axis=(0, 1), keepdims=True)


def row_tiles(count):
    step = 8 if count % 8 == 0 else count
    return [(start, step) for start in range(0, count, step)]


def send_start_kernel(depth, start_ref, maps_ref, row_table, col_table, out_ref):
    blocks, _, width = out_ref.shape
    height = start_ref.shape[3]
    step = height // blocks
    real, imag = start_ref[0, 0], start_ref[0, 1]
    map_real, map_imag = maps_ref[0, 0], maps_ref[0, 1]
    seen_real = (map_real * real - map_imag * imag).reshape(depth * height, width)
    seen_imag = (map_real * imag + map_imag * real).reshape(depth * height, width)
    along_y = rows_times_table(jnp.concatenate([seen_real, seen_imag], axis=1), row_table)
    columns = jnp.concatenate(
        [
            jnp.concatenate(
                [
                    along_y[z * height : (z + 1) * height, part * width : (part + 1) * width]
                    for z in range(depth)
                ],
                axis=1,
            )
            for part in range(2)
        ],
        axis=0,
    )
    spectrum = table_times_columns(col_table, columns)
    for block in range(blocks):
        for part in range(2):
            for z in range(depth):
                first = part * height + block * step
                out_ref[block, pl.ds((part * depth + z) * step, step), :] = spectrum[
                    first : first + step, z * width : (z + 1) * width
                ]


def sampled_residual_kernel(depth, seen_ref, kspace_ref, mask_ref, out_ref):
    length, step = kspace_ref.shape[2], kspace_ref.shape[3]
    norm = 1.0 / math.sqrt(length)

    def place(part, z, start):
        return z // depth, (part * depth + z % depth) * step + start

    for start, size in row_tiles(step):
        parts = []
        for part in range(2):
            cells = []
            for z in range(length):
                slab, row = place(part, z, start)
                cells.append(seen_ref[slab, pl.ds(row, size), :])
            parts.append(cells)
        real, imag = fourier(parts[0], parts[1], -1.0)
        for z in range(length):
            weight = mask_ref[pl.ds(z, 1), :].astype(F32) * norm
            real[z] = weight * (kspace_ref[0, 0, z, pl.ds(start, size), :] - norm * real[z])
            imag[z] = weight * (kspace_ref[0, 1, z, pl.ds(start, size), :] - norm * imag[z])
        real, imag = fourier(real, imag, 1.0)
        for part, cells in enumerate((real, imag)):
            for z in range(length):
                slab, row = place(part, z, start)
                out_ref[slab, pl.ds(row, size), :] = cells[z]


def residual_kernel(
    depth,
    back_ref,
    start_ref,
    dual_ref,
    consensus_ref,
    maps_ref,
    row_table,
    col_table,
    residual_ref,
    send_ref,
    unseen_ref,
):
    blocks, _, width = back_ref.shape
    height = start_ref.shape[3]
    step = height // blocks
    columns = jnp.concatenate(
        [
            jnp.concatenate(
                [back_ref[block, pl.ds((part * depth + z) * step, step), :] for z in range(depth)],
                axis=1,
            )
            for part in (1, 0)
            for block in range(blocks)
        ],
        axis=0,
    )
    along_x = table_times_columns(col_table, columns)
    rows = jnp.concatenate(
        [
            jnp.concatenate(
                [
                    along_x[part * height : (part + 1) * height, z * width : (z + 1) * width]
                    for part in range(2)
                ],
                axis=1,
            )
            for z in range(depth)
        ],
        axis=0,
    )
    image = rows_times_table(rows, row_table)
    unseen = jnp.zeros((8, width), F32)
    for z in range(depth):
        back_imag = image[z * height : (z + 1) * height, :width]
        back_real = image[z * height : (z + 1) * height, width:]
        map_real, map_imag = maps_ref[0, 0, z], maps_ref[0, 1, z]
        pull_real = consensus_ref[0, z] - dual_ref[0, 0, z] - start_ref[0, 0, z]
        pull_imag = consensus_ref[1, z] - dual_ref[0, 1, z] - start_ref[0, 1, z]
        real = map_real * back_real + map_imag * back_imag + pull_real
        imag = map_real * back_imag - map_imag * back_real + pull_imag
        residual_ref[0, z], residual_ref[1, z] = real, imag
        power = map_real * map_real + map_imag * map_imag
        hidden = jnp.where(power < UNSEEN, real * real + imag * imag, 0.0)
        unseen = unseen + jnp.sum(hidden.reshape(height // 8, 8, width), axis=0)
        for part, plane in enumerate(
            (map_real * real - map_imag * imag, map_real * imag + map_imag * real, power)
        ):
            for block in range(blocks):
                send_ref[block, pl.ds((part * depth + z) * step, step), :] = plane[
                    block * step : (block + 1) * step
                ]
    unseen_ref[...] = unseen


def normal_kernel(depth, seen_ref, unseen_ref, mask_ref, row_table, out_ref, work_ref, held_ref):
    blocks, rows, width = seen_ref.shape
    span = rows // 3
    step = span // depth
    length = depth * blocks
    norm = 1.0 / math.sqrt(length)

    def place(z, start):
        return (z // depth) * span + (z % depth) * step + start

    def gather(ref, part):
        return jnp.concatenate([ref[s, pl.ds(part * span, span), :] for s in range(blocks)], axis=0)

    def weigh(z):
        return mask_ref[pl.ds(z, 1), :].astype(F32) * norm

    seen_real, seen_imag = gather(seen_ref, 0), gather(seen_ref, 1)
    along_y = rows_times_table(jnp.concatenate([seen_real, seen_imag], axis=1), row_table)
    work_ref[0], work_ref[1] = along_y[:, :width], along_y[:, width:]
    sampled = None
    for start, size in row_tiles(step):
        real = [work_ref[0, pl.ds(place(z, start), size), :] for z in range(length)]
        imag = [work_ref[1, pl.ds(place(z, start), size), :] for z in range(length)]
        real, imag = fourier(real, imag, -1.0)
        for z in range(length):
            weight = weigh(z)
            real[z], imag[z] = real[z] * weight, imag[z] * weight
            held_ref[0, pl.ds(place(z, start), size), :] = real[z]
            held_ref[1, pl.ds(place(z, start), size), :] = imag[z]
            term = real[z] * real[z] + imag[z] * imag[z]
            sampled = term if sampled is None else sampled + term
        real, imag = fourier(real, imag, 1.0)
        for z in range(length):
            work_ref[0, pl.ds(place(z, start), size), :] = real[z] * norm
            work_ref[1, pl.ds(place(z, start), size), :] = imag[z] * norm
    image = rows_times_table(jnp.concatenate([work_ref[1], work_ref[0]], axis=1), row_table)
    back_real, back_imag = image[:, width:], image[:, :width]
    for s in range(blocks):
        out_ref[s, pl.ds(0, span), :] = back_real[s * span : (s + 1) * span]
        out_ref[s, pl.ds(span, span), :] = back_imag[s * span : (s + 1) * span]
    power = gather(seen_ref, 2)
    inverse = jnp.where(power < UNSEEN, 0.0, 1.0 / jnp.maximum(power, UNSEEN))
    first = total((seen_real * seen_real + seen_imag * seen_imag) * inverse)
    sampled = total(sampled)
    slope = jnp.where(first > 0.0, sampled / jnp.where(first > 0.0, first, 1.0), 0.0)
    rest_real = power * back_real - slope * seen_real
    rest_imag = power * back_imag - slope * seen_imag
    spread = total((rest_real * rest_real + rest_imag * rest_imag) * inverse)
    along_y = rows_times_table(jnp.concatenate([rest_real, rest_imag], axis=1), row_table)
    work_ref[0], work_ref[1] = along_y[:, :width], along_y[:, width:]
    energy, cross = None, None
    for start, size in row_tiles(step):
        real = [work_ref[0, pl.ds(place(z, start), size), :] for z in range(length)]
        imag = [work_ref[1, pl.ds(place(z, start), size), :] for z in range(length)]
        real, imag = fourier(real, imag, -1.0)
        for z in range(length):
            weight = weigh(z)
            real[z], imag[z] = real[z] * weight, imag[z] * weight
            term = real[z] * real[z] + imag[z] * imag[z]
            other = (
                real[z] * held_ref[0, pl.ds(place(z, start), size), :]
                + imag[z] * held_ref[1, pl.ds(place(z, start), size), :]
            )
            energy = term if energy is None else energy + term
            cross = other if cross is None else cross + other
    line = lax.broadcasted_iota(jnp.int32, (8, width), 0)
    sums = jnp.zeros((8, width), F32)
    shares = (first, sampled, spread, total(energy), total(cross), total(unseen_ref[...]))
    for index, share in enumerate(shares):
        sums = jnp.where(line == index, share, sums)
    for s in range(blocks):
        out_ref[s, pl.ds(2 * span, 8), :] = sums


def combine_kernel(depth, back_ref, residual_ref, maps_ref, start_ref, dual_ref, send_ref):
    blocks, rows, width = back_ref.shape
    span = (rows - 8) // 2
    step = span // depth
    height = start_ref.shape[3]
    parts, _, _ = send_ref.shape
    share = height // parts
    sums = [back_ref[s, pl.ds(2 * span, 8), :] for s in range(blocks)]
    added = functools.reduce(lambda a, b: a + b, sums)
    unseen = added[5:6]
    norm_first = added[0:1] + unseen
    sampled = added[1:2]
    slope = sampled / norm_first
    spread = slope * slope * unseen
    energy = jnp.zeros_like(unseen)
    for shares in sums:
        own, own_sampled = shares[0:1], shares[1:2]
        own_slope = jnp.where(own > 0.0, own_sampled / jnp.where(own > 0.0, own, 1.0), 0.0)
        shift = slope - own_slope
        spread = spread + shares[2:3] + shift * shift * own
        energy = energy + shares[3:4] - 2.0 * shift * shares[4:5] + shift * shift * own_sampled
    alpha_first = norm_first / (norm_first + sampled)
    beta = alpha_first * alpha_first * spread / norm_first
    curve = spread + energy - alpha_first * spread * spread / norm_first
    alpha_second = jnp.where(spread > 0.0, spread / jnp.where(spread > 0.0, curve, 1.0), 0.0)
    along_residual = alpha_first + alpha_second * (alpha_first * slope + beta)
    along_back = -alpha_first * alpha_second
    for z in range(depth):
        for block in range(blocks):
            window = pl.ds(block * step, step)
            back_real = back_ref[block, pl.ds(z * step, step), :] * along_back
            back_imag = back_ref[block, pl.ds(span + z * step, step), :] * along_back
            map_real, map_imag = maps_ref[0, 0, z, window, :], maps_ref[0, 1, z, window, :]
            moves = (
                map_real * back_real + map_imag * back_imag,
                map_real * back_imag - map_imag * back_real,
            )
            for part in range(2):
                value = (
                    start_ref[0, part, z, window, :]
                    + dual_ref[0, part, z, window, :]
                    + along_residual * residual_ref[part, z, window, :]
                    + moves[part]
                )
                size = min(step, share)
                for piece in range(step // size):
                    row = block * step + piece * size
                    target = (part * depth + z) * share + row % share
                    send_ref[row // share, pl.ds(target, size), :] = value[
                        piece * size : (piece + 1) * size
                    ]


def shrink_kernel(depth, all_ref, out_ref):
    coils, rows, width = all_ref.shape
    share = rows // (2 * depth)
    line = lax.broadcasted_iota(jnp.int32, (share, width), 0) % 2
    lane = lax.broadcasted_iota(jnp.int32, (share, width), 1) % 2
    low = (line == 0) & (lane == 0)

    def along_lines(cells):
        near = jnp.where(
            line == 0, pltpu.roll(cells, share - 1, 0), pltpu.roll(cells, 1, 0) - 2.0 * cells
        )
        return (cells + near) * ROOT_HALF

    def along_lanes(cells):
        near = jnp.where(
            lane == 0, pltpu.roll(cells, width - 1, 1), pltpu.roll(cells, 1, 1) - 2.0 * cells
        )
        return (cells + near) * ROOT_HALF

    def mean(part, z):
        cells = all_ref[0, pl.ds((part * depth + z) * share, share), :]
        for coil in range(1, coils):
            cells = cells + all_ref[coil, pl.ds((part * depth + z) * share, share), :]
        return cells * (1.0 / coils)

    for z in range(0, depth, 2):
        bands = []
        for part in range(2):
            first, second = mean(part, z), mean(part, z + 1)
            bands.append(
                [
                    along_lanes(along_lines(band))
                    for band in ((first + second) * ROOT_HALF, (first - second) * ROOT_HALF)
                ]
            )
        kept = [[], []]
        for level in range(2):
            real, imag = bands[0][level], bands[1][level]
            size = jnp.sqrt(real * real + imag * imag)
            factor = jnp.maximum(size - THRESHOLD, 0.0) / jnp.maximum(size, THRESHOLD)
            if level == 0:
                factor = jnp.where(low, 1.0, factor)
            kept[0].append(along_lines(along_lanes(real * factor)))
            kept[1].append(along_lines(along_lanes(imag * factor)))
        for part in range(2):
            base, detail = kept[part]
            out_ref[pl.ds((part * depth + z) * share, share), :] = (base + detail) * ROOT_HALF
            out_ref[pl.ds((part * depth + z + 1) * share, share), :] = (base - detail) * ROOT_HALF


def finish_kernel(depth, shrunk_ref, sum_ref, consensus_ref, dual_ref):
    parts, rows, _ = shrunk_ref.shape
    share = rows // (2 * depth)
    for block in range(parts):
        for part in range(2):
            for z in range(depth):
                row = pl.ds((part * depth + z) * share, share)
                window = pl.ds(block * share, share)
                cells = shrunk_ref[block, row, :]
                consensus_ref[part, z, window, :] = cells
                dual_ref[0, part, z, window, :] = sum_ref[block, row, :] - cells


def call(kernel, depth, name, outs, scratch=()):
    in_vmem = pl.BlockSpec(memory_space=pltpu.VMEM)
    shapes = [jax.ShapeDtypeStruct(shape, F32) for shape in outs]

    def run(*operands):
        return pl.pallas_call(
            functools.partial(kernel, depth),
            name=name,
            out_shape=shapes if len(shapes) > 1 else shapes[0],
            in_specs=[in_vmem] * len(operands),
            out_specs=[in_vmem] * len(shapes) if len(shapes) > 1 else in_vmem,
            scratch_shapes=[pltpu.VMEM(shape, F32) for shape in scratch],
            compiler_params=pltpu.CompilerParams(vmem_limit_bytes=32 << 20),
        )(*operands)

    return run


def per_device(warm_start, scaled_dual, consensus, kspace, coil_maps, line_mask):
    depth, height, width = warm_start.shape[2:]
    slabs, coils = lax.axis_size("slab"), lax.axis_size("coil")
    step = height // slabs
    span = depth * step
    share = height // coils
    row_table = jnp.asarray(dft_table(width))
    col_table = row_table if height == width else jnp.asarray(dft_table(height))

    def exchange(values, axis):
        return lax.all_to_all(values, axis, split_axis=0, concat_axis=0, tiled=True)

    seen = call(send_start_kernel, depth, "send_start", [(slabs, 2 * span, width)])(
        warm_start, coil_maps, row_table, col_table
    )
    seen = exchange(seen, "slab")
    back = call(sampled_residual_kernel, depth, "sampled_residual", [(slabs, 2 * span, width)])(
        seen, kspace, line_mask
    )
    back = exchange(back, "slab")
    residual, seen, unseen = call(
        residual_kernel,
        depth,
        "residual",
        [(2, depth, height, width), (slabs, 3 * span, width), (8, width)],
    )(back, warm_start, scaled_dual, consensus, coil_maps, row_table, col_table)
    seen = exchange(seen, "slab")
    work = (2, slabs * span, width)
    back = call(
        normal_kernel, depth, "normal", [(slabs, 2 * span + 8, width)], (work, work)
    )(seen, unseen, line_mask, row_table)
    back = exchange(back, "slab")
    summed = call(combine_kernel, depth, "combine", [(coils, 2 * depth * share, width)])(
        back, residual, coil_maps, warm_start, scaled_dual
    )
    shared = exchange(summed, "coil")
    shrunk = call(shrink_kernel, depth, "shrink", [(2 * depth * share, width)])(shared)
    shrunk = lax.all_gather(shrunk, "coil", axis=0, tiled=False)
    return tuple(
        call(
            finish_kernel,
            depth,
            "finish",
            [(2, depth, height, width), (1, 2, depth, height, width)],
        )(shrunk, summed)
    )


def solution(mesh):
    placed = (
        P("coil", None, "slab", None, None),
        P("coil", None, "slab", None, None),
        P(None, "slab", None, None),
        P("coil", None, None, "slab", None),
        P("coil", None, "slab", None, None),
        P(),
    )
    return jax.shard_map(
        per_device,
        mesh=mesh,
        in_specs=placed,
        out_specs=(P(None, "slab", None, None), P("coil", None, "slab", None, None)),
        check_vma=False,
    )
```

```python
import functools
import math

import jax
import jax.numpy as jnp
import numpy as np
from jax import lax
from jax.experimental import pallas as pl
from jax.experimental.pallas import tpu as pltpu
from jax.sharding import PartitionSpec as P

THRESHOLD = 0.15
ROOT_HALF = 0.7071067811865476
UNSEEN = 1e-20
F32 = jnp.float32
BF16 = jnp.bfloat16


def dft_table(length):
    index = np.arange(length)
    angles = (np.outer(index, index) % length) * (2.0 * math.pi / length)
    cosine = np.cos(angles) / math.sqrt(length)
    sine = np.sin(angles) / math.sqrt(length)
    whole = np.block([[cosine, sine], [-sine, cosine]]).astype(np.float32)
    high = whole.astype(jnp.bfloat16)
    low = (whole - high.astype(np.float32)).astype(jnp.bfloat16)
    return np.stack([high, low])


def halves(values):
    high = values.astype(BF16)
    return high, (values - high.astype(F32)).astype(BF16)


def contract(left, right, dims):
    return lax.dot_general(left, right, (dims, ((), ())), preferred_element_type=F32)


def rows_times_table(values, table_ref):
    high, low = halves(values)
    dims = ((1,), (1,))
    return (
        contract(high, table_ref[0], dims)
        + contract(high, table_ref[1], dims)
        + contract(low, table_ref[0], dims)
    )


def table_times_columns(table_ref, values):
    high, low = halves(values)
    dims = ((1,), (0,))
    return (
        contract(table_ref[0], high, dims)
        + contract(table_ref[1], high, dims)
        + contract(table_ref[0], low, dims)
    )


def fourier(real, imag, sign):
    count = len(real)
    if count == 1:
        return list(real), list(imag)
    if count % 2:
        out_real, out_imag = [], []
        for k in range(count):
            sum_real, sum_imag = real[0], imag[0]
            for n in range(1, count):
                angle = sign * 2.0 * math.pi * (k * n % count) / count
                c, s = math.cos(angle), math.sin(angle)
                sum_real = sum_real + (c * real[n] - s * imag[n])
                sum_imag = sum_imag + (c * imag[n] + s * real[n])
            out_real.append(sum_real)
            out_imag.append(sum_imag)
        return out_real, out_imag
    even_real, even_imag = fourier(real[0::2], imag[0::2], sign)
    odd_real, odd_imag = fourier(real[1::2], imag[1::2], sign)
    half = count // 2
    out_real, out_imag = [None] * count, [None] * count
    for k in range(half):
        x, y = odd_real[k], odd_imag[k]
        if k == 0:
            pass
        elif 4 * k == count:
            x, y = (-y, x) if sign > 0 else (y, -x)
        elif 8 * k == count:
            x, y = (x - sign * y) * ROOT_HALF, (y + sign * x) * ROOT_HALF
        elif 8 * k == 3 * count:
            x, y = (-x - sign * y) * ROOT_HALF, (sign * x - y) * ROOT_HALF
        else:
            angle = sign * 2.0 * math.pi * k / count
            c, s = math.cos(angle), math.sin(angle)
            x, y = c * x - s * y, c * y + s * x
        out_real[k], out_imag[k] = even_real[k] + x, even_imag[k] + y
        out_real[k + half], out_imag[k + half] = even_real[k] - x, even_imag[k] - y
    return out_real, out_imag


def total(values):
    return jnp.sum(values, axis=(0, 1), keepdims=True)


def row_tiles(count):
    step = 8 if count % 8 == 0 else count
    return [(start, step) for start in range(0, count, step)]


def placement():
    index = lax.axis_index("slab")
    return index >> 1, index & 1


def row_of(index, size):
    return pl.ds(pl.multiple_of(index * size, size), size)


def routes(chips):
    return [(k, j) for k in range(chips - 1, -1, -1) for j in range(2)]


def arrivals(chips, refs):
    chip, core = placement()
    return [
        (2 * (chip ^ k) + (core ^ j), ref) for (k, j), ref in zip(routes(chips), refs[: 2 * chips])
    ]


def departures(refs):
    chip, core = placement()
    return [
        (2 * (chip ^ k) + (core ^ j), ref.at[j]) for k, ref in enumerate(refs) for j in range(2)
    ]


def send_start_kernel(depth, start_hbm, maps_hbm, row_hbm, col_hbm, *refs):
    out_refs, (start_ref, maps_ref, row_table, col_table, work_ref, sems) = refs[:-6], refs[-6:]
    fetches = [
        pltpu.make_async_copy(source, target, sems.at[index])
        for index, (source, target) in enumerate(
            (
                (start_hbm, start_ref),
                (maps_hbm, maps_ref),
                (row_hbm, row_table),
                (col_hbm, col_table),
            )
        )
    ]
    for fetch in fetches:
        fetch.start()
    for fetch in fetches:
        fetch.wait()
    _, rows, width = out_refs[0].shape
    height = start_ref.shape[3]
    step = rows // (2 * depth)
    real, imag = start_ref[0, 0], start_ref[0, 1]
    map_real, map_imag = maps_ref[0, 0], maps_ref[0, 1]
    seen_real = (map_real * real - map_imag * imag).reshape(depth * height, width)
    seen_imag = (map_real * imag + map_imag * real).reshape(depth * height, width)
    along_y = rows_times_table(jnp.concatenate([seen_real, seen_imag], axis=1), row_table)
    columns = jnp.concatenate(
        [
            jnp.concatenate(
                [
                    along_y[z * height : (z + 1) * height, part * width : (part + 1) * width]
                    for z in range(depth)
                ],
                axis=1,
            )
            for part in range(2)
        ],
        axis=0,
    )
    spectrum = table_times_columns(col_table, columns)
    for part in range(2):
        for block in range(height // step):
            first = part * height + block * step
            work_ref[part, block] = spectrum[first : first + step]
    for block, out_ref in departures(out_refs):
        for part in range(2):
            for z in range(depth):
                out_ref[pl.ds((part * depth + z) * step, step), :] = work_ref[
                    part, block, :, z * width : (z + 1) * width
                ]


def sampled_residual_kernel(depth, chips, *refs):
    kspace_ref, mask_ref = refs[2 * chips : 2 * chips + 2]
    out_refs, work_ref = refs[2 * chips + 2 : -1], refs[-1]
    length, step = kspace_ref.shape[2], kspace_ref.shape[3]
    span = depth * step
    norm = 1.0 / math.sqrt(length)
    for slab, source in arrivals(chips, refs):
        for part in range(2):
            work_ref[part, row_of(slab, span), :] = source[0, pl.ds(part * span, span), :]
    for start, size in row_tiles(step):
        rows = [pl.ds(z * step + start, size) for z in range(length)]
        real = [work_ref[0, row, :] for row in rows]
        imag = [work_ref[1, row, :] for row in rows]
        real, imag = fourier(real, imag, -1.0)
        for z in range(length):
            weight = mask_ref[pl.ds(z, 1), :].astype(F32) * norm
            real[z] = weight * (kspace_ref[0, 0, z, pl.ds(start, size), :] - norm * real[z])
            imag[z] = weight * (kspace_ref[0, 1, z, pl.ds(start, size), :] - norm * imag[z])
        real, imag = fourier(real, imag, 1.0)
        for z, row in enumerate(rows):
            work_ref[0, row, :], work_ref[1, row, :] = real[z], imag[z]
    for slab, out_ref in departures(out_refs):
        for part in range(2):
            out_ref[pl.ds(part * span, span), :] = work_ref[part, row_of(slab, span), :]


def residual_kernel(depth, chips, *refs):
    (start_ref, dual_ref, consensus_ref, maps_ref, row_table, col_table) = refs[
        2 * chips : 2 * chips + 6
    ]
    residual_ref, unseen_ref = refs[2 * chips + 6 : 2 * chips + 8]
    send_refs, (work_ref, plane_ref) = refs[2 * chips + 8 : -2], refs[-2:]
    _, rows, width = refs[0].shape
    height = start_ref.shape[3]
    step = rows // (2 * depth)
    for block, source in arrivals(chips, refs):
        for part in range(2):
            for z in range(depth):
                work_ref[part, block, :, z * width : (z + 1) * width] = source[
                    0, pl.ds((part * depth + z) * step, step), :
                ]
    blocks = height // step
    columns = jnp.concatenate(
        [work_ref[part, block] for part in (1, 0) for block in range(blocks)], axis=0
    )
    along_x = table_times_columns(col_table, columns)
    rows = jnp.concatenate(
        [
            jnp.concatenate(
                [
                    along_x[part * height : (part + 1) * height, z * width : (z + 1) * width]
                    for part in range(2)
                ],
                axis=1,
            )
            for z in range(depth)
        ],
        axis=0,
    )
    image = rows_times_table(rows, row_table)
    unseen = jnp.zeros((8, width), F32)
    for z in range(depth):
        back_imag = image[z * height : (z + 1) * height, :width]
        back_real = image[z * height : (z + 1) * height, width:]
        map_real, map_imag = maps_ref[0, 0, z], maps_ref[0, 1, z]
        pull_real = consensus_ref[0, z] - dual_ref[0, 0, z] - start_ref[0, 0, z]
        pull_imag = consensus_ref[1, z] - dual_ref[0, 1, z] - start_ref[0, 1, z]
        real = map_real * back_real + map_imag * back_imag + pull_real
        imag = map_real * back_imag - map_imag * back_real + pull_imag
        residual_ref[0, z], residual_ref[1, z] = real, imag
        power = map_real * map_real + map_imag * map_imag
        hidden = jnp.where(power < UNSEEN, real * real + imag * imag, 0.0)
        unseen = unseen + jnp.sum(hidden.reshape(height // 8, 8, width), axis=0)
        for part, plane in enumerate(
            (map_real * real - map_imag * imag, map_real * imag + map_imag * real, power)
        ):
            for block in range(blocks):
                plane_ref[part, z, block] = plane[block * step : (block + 1) * step]
    unseen_ref[...] = unseen
    for block, send_ref in departures(send_refs):
        for part in range(3):
            for z in range(depth):
                send_ref[pl.ds((part * depth + z) * step, step), :] = plane_ref[part, z, block]


def normal_kernel(depth, chips, *refs):
    unseen_ref, mask_ref, row_table = refs[2 * chips : 2 * chips + 3]
    out_refs, (seen_ref, work_ref, held_ref) = refs[2 * chips + 3 : -3], refs[-3:]
    _, rows, width = refs[0].shape
    span = rows // 3
    step = span // depth
    length = depth * chips * 2
    norm = 1.0 / math.sqrt(length)
    for slab, source in arrivals(chips, refs):
        for part in range(3):
            seen_ref[part, row_of(slab, span), :] = source[0, pl.ds(part * span, span), :]

    def place(z, start):
        return z * step + start

    def weigh(z):
        return mask_ref[pl.ds(z, 1), :].astype(F32) * norm

    seen_real, seen_imag = seen_ref[0], seen_ref[1]
    along_y = rows_times_table(jnp.concatenate([seen_real, seen_imag], axis=1), row_table)
    work_ref[0], work_ref[1] = along_y[:, :width], along_y[:, width:]
    sampled = None
    for start, size in row_tiles(step):
        real = [work_ref[0, pl.ds(place(z, start), size), :] for z in range(length)]
        imag = [work_ref[1, pl.ds(place(z, start), size), :] for z in range(length)]
        real, imag = fourier(real, imag, -1.0)
        for z in range(length):
            weight = weigh(z)
            real[z], imag[z] = real[z] * weight, imag[z] * weight
            held_ref[0, pl.ds(place(z, start), size), :] = real[z]
            held_ref[1, pl.ds(place(z, start), size), :] = imag[z]
            term = real[z] * real[z] + imag[z] * imag[z]
            sampled = term if sampled is None else sampled + term
        real, imag = fourier(real, imag, 1.0)
        for z in range(length):
            work_ref[0, pl.ds(place(z, start), size), :] = real[z] * norm
            work_ref[1, pl.ds(place(z, start), size), :] = imag[z] * norm
    image = rows_times_table(jnp.concatenate([work_ref[1], work_ref[0]], axis=1), row_table)
    back_real, back_imag = image[:, width:], image[:, :width]
    work_ref[0], work_ref[1] = back_real, back_imag
    for slab, out_ref in departures(out_refs):
        for part in range(2):
            out_ref[pl.ds(part * span, span), :] = work_ref[part, row_of(slab, span), :]
    power = seen_ref[2]
    inverse = jnp.where(power < UNSEEN, 0.0, 1.0 / jnp.maximum(power, UNSEEN))
    first = total((seen_real * seen_real + seen_imag * seen_imag) * inverse)
    sampled = total(sampled)
    slope = jnp.where(first > 0.0, sampled / jnp.where(first > 0.0, first, 1.0), 0.0)
    rest_real = power * back_real - slope * seen_real
    rest_imag = power * back_imag - slope * seen_imag
    spread = total((rest_real * rest_real + rest_imag * rest_imag) * inverse)
    along_y = rows_times_table(jnp.concatenate([rest_real, rest_imag], axis=1), row_table)
    work_ref[0], work_ref[1] = along_y[:, :width], along_y[:, width:]
    energy, cross = None, None
    for start, size in row_tiles(step):
        real = [work_ref[0, pl.ds(place(z, start), size), :] for z in range(length)]
        imag = [work_ref[1, pl.ds(place(z, start), size), :] for z in range(length)]
        real, imag = fourier(real, imag, -1.0)
        for z in range(length):
            weight = weigh(z)
            real[z], imag[z] = real[z] * weight, imag[z] * weight
            term = real[z] * real[z] + imag[z] * imag[z]
            other_term = (
                real[z] * held_ref[0, pl.ds(place(z, start), size), :]
                + imag[z] * held_ref[1, pl.ds(place(z, start), size), :]
            )
            energy = term if energy is None else energy + term
            cross = other_term if cross is None else cross + other_term
    line = lax.broadcasted_iota(jnp.int32, (8, width), 0)
    sums = jnp.zeros((8, width), F32)
    shares = (first, sampled, spread, total(energy), total(cross), total(unseen_ref[...]))
    for index, share in enumerate(shares):
        sums = jnp.where(line == index, share, sums)
    for out_ref in out_refs:
        for j in range(2):
            out_ref[j, pl.ds(2 * span, 8), :] = sums


def combine_kernel(depth, chips, *refs):
    residual_ref, maps_ref, start_ref, dual_ref = refs[2 * chips : 2 * chips + 4]
    send_refs, sum_ref, back_ref = refs[2 * chips + 4 : -2], refs[-2], refs[-1]
    _, rows, width = refs[0].shape
    span = (rows - 8) // 2
    step = span // depth
    height = start_ref.shape[3]
    parts = len(send_refs)
    share = height // parts
    sources = arrivals(chips, refs)
    sums = [source[0, pl.ds(2 * span, 8), :] for _, source in sources]
    added = functools.reduce(lambda a, b: a + b, sums)
    unseen = added[5:6]
    norm_first = added[0:1] + unseen
    sampled = added[1:2]
    slope = sampled / norm_first
    spread = slope * slope * unseen
    energy = jnp.zeros_like(unseen)
    for shares in sums:
        own, own_sampled = shares[0:1], shares[1:2]
        own_slope = jnp.where(own > 0.0, own_sampled / jnp.where(own > 0.0, own, 1.0), 0.0)
        shift = slope - own_slope
        spread = spread + shares[2:3] + shift * shift * own
        energy = energy + shares[3:4] - 2.0 * shift * shares[4:5] + shift * shift * own_sampled
    alpha_first = norm_first / (norm_first + sampled)
    beta = alpha_first * alpha_first * spread / norm_first
    curve = spread + energy - alpha_first * spread * spread / norm_first
    alpha_second = jnp.where(spread > 0.0, spread / jnp.where(spread > 0.0, curve, 1.0), 0.0)
    along_residual = alpha_first + alpha_second * (alpha_first * slope + beta)
    along_back = -alpha_first * alpha_second
    for block, source in sources:
        for part in range(2):
            for z in range(depth):
                back_ref[part, z, block] = source[0, pl.ds(part * span + z * step, step), :]
    for block in range(height // step):
        window = pl.ds(block * step, step)
        for z in range(depth):
            back_real = back_ref[0, z, block] * along_back
            back_imag = back_ref[1, z, block] * along_back
            map_real, map_imag = maps_ref[0, 0, z, window, :], maps_ref[0, 1, z, window, :]
            moves = (
                map_real * back_real + map_imag * back_imag,
                map_real * back_imag - map_imag * back_real,
            )
            for part in range(2):
                sum_ref[part, z, window, :] = (
                    start_ref[0, part, z, window, :]
                    + dual_ref[0, part, z, window, :]
                    + along_residual * residual_ref[part, z, window, :]
                    + moves[part]
                )
    coil = lax.axis_index("coil")
    for k in range(parts):
        window = row_of(coil ^ k, share)
        for part in range(2):
            for z in range(depth):
                send_refs[k][pl.ds((part * depth + z) * share, share), :] = sum_ref[
                    part, z, window, :
                ]


def shrink_kernel(depth, *refs):
    all_refs, out_ref = refs[:-1], refs[-1]
    coils = len(all_refs)
    rows, width = out_ref.shape
    share = rows // (2 * depth)
    line = lax.broadcasted_iota(jnp.int32, (share, width), 0) % 2
    lane = lax.broadcasted_iota(jnp.int32, (share, width), 1) % 2
    low = (line == 0) & (lane == 0)

    def along_lines(cells):
        near = jnp.where(
            line == 0, pltpu.roll(cells, share - 1, 0), pltpu.roll(cells, 1, 0) - 2.0 * cells
        )
        return (cells + near) * ROOT_HALF

    def along_lanes(cells):
        near = jnp.where(
            lane == 0, pltpu.roll(cells, width - 1, 1), pltpu.roll(cells, 1, 1) - 2.0 * cells
        )
        return (cells + near) * ROOT_HALF

    def mean(part, z):
        window = pl.ds((part * depth + z) * share, share)
        return functools.reduce(lambda a, b: a + b, [ref[window, :] for ref in all_refs]) * (
            1.0 / coils
        )

    for z in range(0, depth, 2):
        bands = []
        for part in range(2):
            first, second = mean(part, z), mean(part, z + 1)
            bands.append(
                [
                    along_lanes(along_lines(band))
                    for band in ((first + second) * ROOT_HALF, (first - second) * ROOT_HALF)
                ]
            )
        kept = [[], []]
        for level in range(2):
            real, imag = bands[0][level], bands[1][level]
            size = jnp.sqrt(real * real + imag * imag)
            factor = jnp.maximum(size - THRESHOLD, 0.0) / jnp.maximum(size, THRESHOLD)
            if level == 0:
                factor = jnp.where(low, 1.0, factor)
            kept[0].append(along_lines(along_lanes(real * factor)))
            kept[1].append(along_lines(along_lanes(imag * factor)))
        for part in range(2):
            base, detail = kept[part]
            out_ref[pl.ds((part * depth + z) * share, share), :] = (base + detail) * ROOT_HALF
            out_ref[pl.ds((part * depth + z + 1) * share, share), :] = (base - detail) * ROOT_HALF


def finish_kernel(depth, *refs):
    parts = len(refs) - 3
    sum_ref, consensus_ref, dual_ref = refs[parts:]
    share = refs[0].shape[0] // (2 * depth)
    coil = lax.axis_index("coil")
    for k in range(parts):
        window = row_of(coil ^ k, share)
        for part in range(2):
            for z in range(depth):
                cells = refs[k][pl.ds((part * depth + z) * share, share), :]
                consensus_ref[part, z, window, :] = cells
                dual_ref[0, part, z, window, :] = sum_ref[part, z, window, :] - cells


def call(kernel, name, outs, scratch=(), fetched=False):
    in_vmem = pl.BlockSpec(memory_space=pltpu.VMEM)
    left = pl.BlockSpec(memory_space=pltpu.HBM)
    shapes = [jax.ShapeDtypeStruct(shape, F32) for shape in outs]

    def run(*operands):
        return pl.pallas_call(
            kernel,
            name=name,
            out_shape=shapes if len(shapes) > 1 else shapes[0],
            in_specs=[left if fetched else in_vmem] * len(operands),
            out_specs=[in_vmem] * len(shapes) if len(shapes) > 1 else in_vmem,
            scratch_shapes=[pltpu.VMEM(s, F32) if isinstance(s, tuple) else s for s in scratch],
            compiler_params=pltpu.CompilerParams(vmem_limit_bytes=32 << 20),
        )(*operands)

    return run


def spread_over(axis, size, mask):
    return lambda values: lax.ppermute(values, axis, [(i, i ^ mask) for i in range(size)])


def per_device(warm_start, scaled_dual, consensus, kspace, coil_maps, line_mask):
    depth, height, width = warm_start.shape[2:]
    slabs, coils = lax.axis_size("slab"), lax.axis_size("coil")
    chips = slabs // 2
    step = height // slabs
    span = depth * step
    share = height // coils
    row_table = jnp.asarray(dft_table(width))
    col_table = row_table if height == width else jnp.asarray(dft_table(height))
    tables = (row_table, col_table)
    table_shapes = [pltpu.VMEM(table.shape, BF16) for table in tables]
    image = (2, depth, height, width)

    def exchange(pieces):
        return [
            spread_over("slab", slabs, 2 * k + j)(pieces[k][j : j + 1]) if k + j else pieces[0]
            for k, j in routes(chips)
        ]

    piece = (2, 2 * span, width)
    seen = call(
        functools.partial(send_start_kernel, depth),
        "send_start",
        [piece] * chips,
        [
            warm_start.shape,
            coil_maps.shape,
            *table_shapes,
            (2, slabs, step, depth * width),
            pltpu.SemaphoreType.DMA((4,)),
        ],
        fetched=True,
    )(*(pltpu.with_memory_space_constraint(a, pltpu.HBM) for a in (warm_start, coil_maps, *tables)))
    back = call(
        functools.partial(sampled_residual_kernel, depth, chips),
        "sampled_residual",
        [piece] * chips,
        [(2, slabs * span, width)],
    )(*exchange(seen), kspace, line_mask)
    residual, unseen, *seen = call(
        functools.partial(residual_kernel, depth, chips),
        "residual",
        [image, (8, width)] + [(2, 3 * span, width)] * chips,
        [(2, slabs, step, depth * width), (3, depth, slabs, step, width)],
    )(*exchange(back), warm_start, scaled_dual, consensus, coil_maps, *tables)
    back = call(
        functools.partial(normal_kernel, depth, chips),
        "normal",
        [(2, 2 * span + 8, width)] * chips,
        [(parts, slabs * span, width) for parts in (3, 2, 2)],
    )(*exchange(seen), unseen, line_mask, row_table)
    *shares, summed = call(
        functools.partial(combine_kernel, depth, chips),
        "combine",
        [(2 * depth * share, width)] * coils + [image],
        [(2, depth, slabs, step, width)],
    )(*exchange(back), residual, coil_maps, warm_start, scaled_dual)
    shares = [
        values if k == 0 else spread_over("coil", coils, k)(values)
        for k, values in reversed(list(enumerate(shares)))
    ]
    shrunk = call(
        functools.partial(shrink_kernel, depth), "shrink", [(2 * depth * share, width)]
    )(*shares)
    shrunk = [
        shrunk if k == 0 else spread_over("coil", coils, k)(shrunk) for k in range(coils)
    ]
    return tuple(
        call(functools.partial(finish_kernel, depth), "finish", [image, (1, *image)])(
            *shrunk, summed
        )
    )


def solution(mesh):
    placed = (
        P("coil", None, "slab", None, None),
        P("coil", None, "slab", None, None),
        P(None, "slab", None, None),
        P("coil", None, None, "slab", None),
        P("coil", None, "slab", None, None),
        P(),
    )
    return jax.shard_map(
        per_device,
        mesh=mesh,
        in_specs=placed,
        out_specs=(P(None, "slab", None, None), P("coil", None, "slab", None, None)),
        check_vma=False,
    )
```

```python
import functools
import math

import jax
import jax.numpy as jnp
import numpy as np
from jax import lax
from jax.experimental import pallas as pl
from jax.experimental.pallas import tpu as pltpu
from jax.sharding import PartitionSpec as P

THRESHOLD = 0.15
ROOT_HALF = 0.7071067811865476
UNSEEN = 1e-20
F32 = jnp.float32
BF16 = jnp.bfloat16


def dft_table(length):
    index = np.arange(length)
    angles = (np.outer(index, index) % length) * (2.0 * math.pi / length)
    cosine = np.cos(angles) / math.sqrt(length)
    sine = np.sin(angles) / math.sqrt(length)
    whole = np.block([[cosine, sine], [-sine, cosine]]).astype(np.float32)
    high = whole.astype(jnp.bfloat16)
    low = (whole - high.astype(np.float32)).astype(jnp.bfloat16)
    return np.stack([high, low])


def halves(values):
    high = values.astype(BF16)
    return high, (values - high.astype(F32)).astype(BF16)


def contract(left, right, dims):
    return lax.dot_general(left, right, (dims, ((), ())), preferred_element_type=F32)


def rows_times_table(values, table_ref):
    high, low = halves(values)
    dims = ((1,), (1,))
    return (
        contract(high, table_ref[0], dims)
        + contract(high, table_ref[1], dims)
        + contract(low, table_ref[0], dims)
    )


def table_times_columns(table_ref, values):
    high, low = halves(values)
    dims = ((1,), (0,))
    return (
        contract(table_ref[0], high, dims)
        + contract(table_ref[1], high, dims)
        + contract(table_ref[0], low, dims)
    )


def fourier(real, imag, sign):
    count = len(real)
    if count == 1:
        return list(real), list(imag)
    if count % 2:
        out_real, out_imag = [], []
        for k in range(count):
            sum_real, sum_imag = real[0], imag[0]
            for n in range(1, count):
                angle = sign * 2.0 * math.pi * (k * n % count) / count
                c, s = math.cos(angle), math.sin(angle)
                sum_real = sum_real + (c * real[n] - s * imag[n])
                sum_imag = sum_imag + (c * imag[n] + s * real[n])
            out_real.append(sum_real)
            out_imag.append(sum_imag)
        return out_real, out_imag
    even_real, even_imag = fourier(real[0::2], imag[0::2], sign)
    odd_real, odd_imag = fourier(real[1::2], imag[1::2], sign)
    half = count // 2
    out_real, out_imag = [None] * count, [None] * count
    for k in range(half):
        x, y = odd_real[k], odd_imag[k]
        if k == 0:
            pass
        elif 4 * k == count:
            x, y = (-y, x) if sign > 0 else (y, -x)
        elif 8 * k == count:
            x, y = (x - sign * y) * ROOT_HALF, (y + sign * x) * ROOT_HALF
        elif 8 * k == 3 * count:
            x, y = (-x - sign * y) * ROOT_HALF, (sign * x - y) * ROOT_HALF
        else:
            angle = sign * 2.0 * math.pi * k / count
            c, s = math.cos(angle), math.sin(angle)
            x, y = c * x - s * y, c * y + s * x
        out_real[k], out_imag[k] = even_real[k] + x, even_imag[k] + y
        out_real[k + half], out_imag[k + half] = even_real[k] - x, even_imag[k] - y
    return out_real, out_imag


def total(values):
    return jnp.sum(values, axis=(0, 1), keepdims=True)


def row_tiles(count):
    step = 8 if count % 8 == 0 else count
    return [(start, step) for start in range(0, count, step)]


def placement():
    index = lax.axis_index("slab")
    return index >> 1, index & 1


def row_of(index, size):
    return pl.ds(pl.multiple_of(index * size, size), size)


def passed_on(chips, k):
    return 2 * k > chips


def routes(chips):
    far = [k for k in range(chips - 1, 0, -1) if passed_on(chips, k)]
    near = [k for k in range(chips - 1, 0, -1) if not passed_on(chips, k)]
    return (
        [(k, 0) for k in far]
        + [(k, j) for k in near for j in range(2)]
        + [(0, 0), (0, 1)]
        + [(k, 1) for k in far[::-1]]
    )


def arrivals(chips, refs):
    chip, core = placement()
    return [
        (2 * (chip ^ k) + (core ^ j), ref) for (k, j), ref in zip(routes(chips), refs[: 2 * chips])
    ]


def departures(refs):
    chip, core = placement()
    return [
        (2 * (chip ^ k) + (core ^ j), ref.at[j]) for k, ref in enumerate(refs) for j in range(2)
    ]


def send_start_kernel(depth, start_hbm, maps_hbm, row_hbm, col_hbm, *refs):
    out_refs, (start_ref, maps_ref, row_table, col_table, work_ref, sems) = refs[:-6], refs[-6:]
    fetches = [
        pltpu.make_async_copy(source, target, sems.at[index])
        for index, (source, target) in enumerate(
            (
                (start_hbm, start_ref),
                (maps_hbm, maps_ref),
                (row_hbm, row_table),
                (col_hbm, col_table),
            )
        )
    ]
    for fetch in fetches:
        fetch.start()
    for fetch in fetches:
        fetch.wait()
    _, rows, width = out_refs[0].shape
    height = start_ref.shape[3]
    step = rows // (2 * depth)
    real, imag = start_ref[0, 0], start_ref[0, 1]
    map_real, map_imag = maps_ref[0, 0], maps_ref[0, 1]
    seen_real = (map_real * real - map_imag * imag).reshape(depth * height, width)
    seen_imag = (map_real * imag + map_imag * real).reshape(depth * height, width)
    along_y = rows_times_table(jnp.concatenate([seen_real, seen_imag], axis=1), row_table)
    columns = jnp.concatenate(
        [
            jnp.concatenate(
                [
                    along_y[z * height : (z + 1) * height, part * width : (part + 1) * width]
                    for z in range(depth)
                ],
                axis=1,
            )
            for part in range(2)
        ],
        axis=0,
    )
    spectrum = table_times_columns(col_table, columns)
    for part in range(2):
        for block in range(height // step):
            first = part * height + block * step
            work_ref[part, block] = spectrum[first : first + step]
    for block, out_ref in departures(out_refs):
        for part in range(2):
            for z in range(depth):
                out_ref[pl.ds((part * depth + z) * step, step), :] = work_ref[
                    part, block, :, z * width : (z + 1) * width
                ]


def sampled_residual_kernel(depth, chips, *refs):
    kspace_ref, mask_ref = refs[2 * chips : 2 * chips + 2]
    out_refs, work_ref = refs[2 * chips + 2 : -1], refs[-1]
    length, step = kspace_ref.shape[2], kspace_ref.shape[3]
    span = depth * step
    norm = 1.0 / math.sqrt(length)
    for slab, source in arrivals(chips, refs):
        for part in range(2):
            work_ref[part, row_of(slab, span), :] = source[0, pl.ds(part * span, span), :]
    for start, size in row_tiles(step):
        rows = [pl.ds(z * step + start, size) for z in range(length)]
        real = [work_ref[0, row, :] for row in rows]
        imag = [work_ref[1, row, :] for row in rows]
        real, imag = fourier(real, imag, -1.0)
        for z in range(length):
            weight = mask_ref[pl.ds(z, 1), :].astype(F32) * norm
            real[z] = weight * (kspace_ref[0, 0, z, pl.ds(start, size), :] - norm * real[z])
            imag[z] = weight * (kspace_ref[0, 1, z, pl.ds(start, size), :] - norm * imag[z])
        real, imag = fourier(real, imag, 1.0)
        for z, row in enumerate(rows):
            work_ref[0, row, :], work_ref[1, row, :] = real[z], imag[z]
    for slab, out_ref in departures(out_refs):
        for part in range(2):
            out_ref[pl.ds(part * span, span), :] = work_ref[part, row_of(slab, span), :]


def residual_kernel(depth, chips, *refs):
    (start_ref, dual_ref, consensus_ref, maps_ref, row_table, col_table) = refs[
        2 * chips : 2 * chips + 6
    ]
    residual_ref, unseen_ref = refs[2 * chips + 6 : 2 * chips + 8]
    send_refs, (work_ref, plane_ref) = refs[2 * chips + 8 : -2], refs[-2:]
    _, rows, width = refs[0].shape
    height = start_ref.shape[3]
    step = rows // (2 * depth)
    for block, source in arrivals(chips, refs):
        for part in range(2):
            for z in range(depth):
                work_ref[part, block, :, z * width : (z + 1) * width] = source[
                    0, pl.ds((part * depth + z) * step, step), :
                ]
    blocks = height // step
    columns = jnp.concatenate(
        [work_ref[part, block] for part in (1, 0) for block in range(blocks)], axis=0
    )
    along_x = table_times_columns(col_table, columns)
    rows = jnp.concatenate(
        [
            jnp.concatenate(
                [
                    along_x[part * height : (part + 1) * height, z * width : (z + 1) * width]
                    for part in range(2)
                ],
                axis=1,
            )
            for z in range(depth)
        ],
        axis=0,
    )
    image = rows_times_table(rows, row_table)
    unseen = jnp.zeros((8, width), F32)
    for z in range(depth):
        back_imag = image[z * height : (z + 1) * height, :width]
        back_real = image[z * height : (z + 1) * height, width:]
        map_real, map_imag = maps_ref[0, 0, z], maps_ref[0, 1, z]
        pull_real = consensus_ref[0, z] - dual_ref[0, 0, z] - start_ref[0, 0, z]
        pull_imag = consensus_ref[1, z] - dual_ref[0, 1, z] - start_ref[0, 1, z]
        real = map_real * back_real + map_imag * back_imag + pull_real
        imag = map_real * back_imag - map_imag * back_real + pull_imag
        residual_ref[0, z], residual_ref[1, z] = real, imag
        power = map_real * map_real + map_imag * map_imag
        hidden = jnp.where(power < UNSEEN, real * real + imag * imag, 0.0)
        unseen = unseen + jnp.sum(hidden.reshape(height // 8, 8, width), axis=0)
        for part, plane in enumerate(
            (map_real * real - map_imag * imag, map_real * imag + map_imag * real, power)
        ):
            for block in range(blocks):
                plane_ref[part, z, block] = plane[block * step : (block + 1) * step]
    unseen_ref[...] = unseen
    for block, send_ref in departures(send_refs):
        for part in range(3):
            for z in range(depth):
                send_ref[pl.ds((part * depth + z) * step, step), :] = plane_ref[part, z, block]


def normal_kernel(depth, chips, *refs):
    unseen_ref, mask_ref, row_table = refs[2 * chips : 2 * chips + 3]
    out_refs, (seen_ref, work_ref, held_ref) = refs[2 * chips + 3 : -3], refs[-3:]
    _, rows, width = refs[0].shape
    span = rows // 3
    step = span // depth
    length = depth * chips * 2
    norm = 1.0 / math.sqrt(length)
    for slab, source in arrivals(chips, refs):
        for part in range(3):
            seen_ref[part, row_of(slab, span), :] = source[0, pl.ds(part * span, span), :]

    def place(z, start):
        return z * step + start

    def weigh(z):
        return mask_ref[pl.ds(z, 1), :].astype(F32) * norm

    seen_real, seen_imag = seen_ref[0], seen_ref[1]
    along_y = rows_times_table(jnp.concatenate([seen_real, seen_imag], axis=1), row_table)
    work_ref[0], work_ref[1] = along_y[:, :width], along_y[:, width:]
    sampled = None
    for start, size in row_tiles(step):
        real = [work_ref[0, pl.ds(place(z, start), size), :] for z in range(length)]
        imag = [work_ref[1, pl.ds(place(z, start), size), :] for z in range(length)]
        real, imag = fourier(real, imag, -1.0)
        for z in range(length):
            weight = weigh(z)
            real[z], imag[z] = real[z] * weight, imag[z] * weight
            held_ref[0, pl.ds(place(z, start), size), :] = real[z]
            held_ref[1, pl.ds(place(z, start), size), :] = imag[z]
            term = real[z] * real[z] + imag[z] * imag[z]
            sampled = term if sampled is None else sampled + term
        real, imag = fourier(real, imag, 1.0)
        for z in range(length):
            work_ref[0, pl.ds(place(z, start), size), :] = real[z] * norm
            work_ref[1, pl.ds(place(z, start), size), :] = imag[z] * norm
    image = rows_times_table(jnp.concatenate([work_ref[1], work_ref[0]], axis=1), row_table)
    back_real, back_imag = image[:, width:], image[:, :width]
    work_ref[0], work_ref[1] = back_real, back_imag
    for slab, out_ref in departures(out_refs):
        for part in range(2):
            out_ref[pl.ds(part * span, span), :] = work_ref[part, row_of(slab, span), :]
    power = seen_ref[2]
    inverse = jnp.where(power < UNSEEN, 0.0, 1.0 / jnp.maximum(power, UNSEEN))
    first = total((seen_real * seen_real + seen_imag * seen_imag) * inverse)
    sampled = total(sampled)
    slope = jnp.where(first > 0.0, sampled / jnp.where(first > 0.0, first, 1.0), 0.0)
    rest_real = power * back_real - slope * seen_real
    rest_imag = power * back_imag - slope * seen_imag
    spread = total((rest_real * rest_real + rest_imag * rest_imag) * inverse)
    along_y = rows_times_table(jnp.concatenate([rest_real, rest_imag], axis=1), row_table)
    work_ref[0], work_ref[1] = along_y[:, :width], along_y[:, width:]
    energy, cross = None, None
    for start, size in row_tiles(step):
        real = [work_ref[0, pl.ds(place(z, start), size), :] for z in range(length)]
        imag = [work_ref[1, pl.ds(place(z, start), size), :] for z in range(length)]
        real, imag = fourier(real, imag, -1.0)
        for z in range(length):
            weight = weigh(z)
            real[z], imag[z] = real[z] * weight, imag[z] * weight
            term = real[z] * real[z] + imag[z] * imag[z]
            other_term = (
                real[z] * held_ref[0, pl.ds(place(z, start), size), :]
                + imag[z] * held_ref[1, pl.ds(place(z, start), size), :]
            )
            energy = term if energy is None else energy + term
            cross = other_term if cross is None else cross + other_term
    line = lax.broadcasted_iota(jnp.int32, (8, width), 0)
    sums = jnp.zeros((8, width), F32)
    shares = (first, sampled, spread, total(energy), total(cross), total(unseen_ref[...]))
    for index, share in enumerate(shares):
        sums = jnp.where(line == index, share, sums)
    for out_ref in out_refs:
        for j in range(2):
            out_ref[j, pl.ds(2 * span, 8), :] = sums


def combine_kernel(depth, chips, *refs):
    residual_ref, maps_ref, start_ref, dual_ref = refs[2 * chips : 2 * chips + 4]
    send_refs, sum_ref, back_ref = refs[2 * chips + 4 : -2], refs[-2], refs[-1]
    _, rows, width = refs[0].shape
    span = (rows - 8) // 2
    step = span // depth
    height = start_ref.shape[3]
    parts = len(send_refs)
    share = height // parts
    sources = arrivals(chips, refs)
    sums = [source[0, pl.ds(2 * span, 8), :] for _, source in sources]
    added = functools.reduce(lambda a, b: a + b, sums)
    unseen = added[5:6]
    norm_first = added[0:1] + unseen
    sampled = added[1:2]
    slope = sampled / norm_first
    spread = slope * slope * unseen
    energy = jnp.zeros_like(unseen)
    for shares in sums:
        own, own_sampled = shares[0:1], shares[1:2]
        own_slope = jnp.where(own > 0.0, own_sampled / jnp.where(own > 0.0, own, 1.0), 0.0)
        shift = slope - own_slope
        spread = spread + shares[2:3] + shift * shift * own
        energy = energy + shares[3:4] - 2.0 * shift * shares[4:5] + shift * shift * own_sampled
    alpha_first = norm_first / (norm_first + sampled)
    beta = alpha_first * alpha_first * spread / norm_first
    curve = spread + energy - alpha_first * spread * spread / norm_first
    alpha_second = jnp.where(spread > 0.0, spread / jnp.where(spread > 0.0, curve, 1.0), 0.0)
    along_residual = alpha_first + alpha_second * (alpha_first * slope + beta)
    along_back = -alpha_first * alpha_second
    for block, source in sources:
        for part in range(2):
            for z in range(depth):
                back_ref[part, z, block] = source[0, pl.ds(part * span + z * step, step), :]
    for block in range(height // step):
        window = pl.ds(block * step, step)
        for z in range(depth):
            back_real = back_ref[0, z, block] * along_back
            back_imag = back_ref[1, z, block] * along_back
            map_real, map_imag = maps_ref[0, 0, z, window, :], maps_ref[0, 1, z, window, :]
            moves = (
                map_real * back_real + map_imag * back_imag,
                map_real * back_imag - map_imag * back_real,
            )
            for part in range(2):
                sum_ref[part, z, window, :] = (
                    start_ref[0, part, z, window, :]
                    + dual_ref[0, part, z, window, :]
                    + along_residual * residual_ref[part, z, window, :]
                    + moves[part]
                )
    coil = lax.axis_index("coil")
    for k in range(parts):
        window = row_of(coil ^ k, share)
        for part in range(2):
            for z in range(depth):
                send_refs[k][pl.ds((part * depth + z) * share, share), :] = sum_ref[
                    part, z, window, :
                ]


def shrink_kernel(depth, *refs):
    all_refs, out_ref = refs[:-1], refs[-1]
    coils = len(all_refs)
    rows, width = out_ref.shape
    share = rows // (2 * depth)
    line = lax.broadcasted_iota(jnp.int32, (share, width), 0) % 2
    lane = lax.broadcasted_iota(jnp.int32, (share, width), 1) % 2
    low = (line == 0) & (lane == 0)

    def along_lines(cells):
        near = jnp.where(
            line == 0, pltpu.roll(cells, share - 1, 0), pltpu.roll(cells, 1, 0) - 2.0 * cells
        )
        return (cells + near) * ROOT_HALF

    def along_lanes(cells):
        near = jnp.where(
            lane == 0, pltpu.roll(cells, width - 1, 1), pltpu.roll(cells, 1, 1) - 2.0 * cells
        )
        return (cells + near) * ROOT_HALF

    def mean(part, z):
        window = pl.ds((part * depth + z) * share, share)
        return functools.reduce(lambda a, b: a + b, [ref[window, :] for ref in all_refs]) * (
            1.0 / coils
        )

    for z in range(0, depth, 2):
        bands = []
        for part in range(2):
            first, second = mean(part, z), mean(part, z + 1)
            bands.append(
                [
                    along_lanes(along_lines(band))
                    for band in ((first + second) * ROOT_HALF, (first - second) * ROOT_HALF)
                ]
            )
        kept = [[], []]
        for level in range(2):
            real, imag = bands[0][level], bands[1][level]
            size = jnp.sqrt(real * real + imag * imag)
            factor = jnp.maximum(size - THRESHOLD, 0.0) / jnp.maximum(size, THRESHOLD)
            if level == 0:
                factor = jnp.where(low, 1.0, factor)
            kept[0].append(along_lines(along_lanes(real * factor)))
            kept[1].append(along_lines(along_lanes(imag * factor)))
        for part in range(2):
            base, detail = kept[part]
            out_ref[pl.ds((part * depth + z) * share, share), :] = (base + detail) * ROOT_HALF
            out_ref[pl.ds((part * depth + z + 1) * share, share), :] = (base - detail) * ROOT_HALF


def finish_kernel(depth, *refs):
    parts = len(refs) - 3
    sum_ref, consensus_ref, dual_ref = refs[parts:]
    share = refs[0].shape[0] // (2 * depth)
    coil = lax.axis_index("coil")
    for k in range(parts):
        window = row_of(coil ^ k, share)
        for part in range(2):
            for z in range(depth):
                cells = refs[k][pl.ds((part * depth + z) * share, share), :]
                consensus_ref[part, z, window, :] = cells
                dual_ref[0, part, z, window, :] = sum_ref[part, z, window, :] - cells


def call(kernel, name, outs, scratch=(), fetched=False):
    in_vmem = pl.BlockSpec(memory_space=pltpu.VMEM)
    left = pl.BlockSpec(memory_space=pltpu.HBM)
    shapes = [jax.ShapeDtypeStruct(shape, F32) for shape in outs]

    def run(*operands):
        return pl.pallas_call(
            kernel,
            name=name,
            out_shape=shapes if len(shapes) > 1 else shapes[0],
            in_specs=[left if fetched else in_vmem] * len(operands),
            out_specs=[in_vmem] * len(shapes) if len(shapes) > 1 else in_vmem,
            scratch_shapes=[pltpu.VMEM(s, F32) if isinstance(s, tuple) else s for s in scratch],
            compiler_params=pltpu.CompilerParams(vmem_limit_bytes=32 << 20),
        )(*operands)

    return run


def spread_over(axis, size, mask):
    return lambda values: lax.ppermute(values, axis, [(i, i ^ mask) for i in range(size)])


def per_device(warm_start, scaled_dual, consensus, kspace, coil_maps, line_mask):
    depth, height, width = warm_start.shape[2:]
    slabs, coils = lax.axis_size("slab"), lax.axis_size("coil")
    chips = slabs // 2
    step = height // slabs
    span = depth * step
    share = height // coils
    row_table = jnp.asarray(dft_table(width))
    col_table = row_table if height == width else jnp.asarray(dft_table(height))
    tables = (row_table, col_table)
    table_shapes = [pltpu.VMEM(table.shape, BF16) for table in tables]
    image = (2, depth, height, width)

    def exchange(pieces):
        landed = {(0, 0): pieces[0], (0, 1): spread_over("slab", slabs, 1)(pieces[0][1:2])}
        for k in range(1, chips):
            if passed_on(chips, k):
                landed[k, 0] = spread_over("slab", slabs, 2 * k)(pieces[k])
                landed[k, 1] = spread_over("slab", slabs, 1)(landed[k, 0][1:2])
                continue
            for j in range(2):
                half, _ = lax.optimization_barrier((pieces[k][j : j + 1], landed[0, 1]))
                landed[k, j] = spread_over("slab", slabs, 2 * k + j)(half)
        return [landed[route] for route in routes(chips)]

    piece = (2, 2 * span, width)
    seen = call(
        functools.partial(send_start_kernel, depth),
        "send_start",
        [piece] * chips,
        [
            warm_start.shape,
            coil_maps.shape,
            *table_shapes,
            (2, slabs, step, depth * width),
            pltpu.SemaphoreType.DMA((4,)),
        ],
        fetched=True,
    )(
        *(
            pltpu.with_memory_space_constraint(operand, pltpu.HBM)
            for operand in (warm_start, coil_maps, *tables)
        )
    )
    back = call(
        functools.partial(sampled_residual_kernel, depth, chips),
        "sampled_residual",
        [piece] * chips,
        [(2, slabs * span, width)],
    )(*exchange(seen), kspace, line_mask)
    residual, unseen, *seen = call(
        functools.partial(residual_kernel, depth, chips),
        "residual",
        [image, (8, width)] + [(2, 3 * span, width)] * chips,
        [(2, slabs, step, depth * width), (3, depth, slabs, step, width)],
    )(*exchange(back), warm_start, scaled_dual, consensus, coil_maps, *tables)
    back = call(
        functools.partial(normal_kernel, depth, chips),
        "normal",
        [(2, 2 * span + 8, width)] * chips,
        [(parts, slabs * span, width) for parts in (3, 2, 2)],
    )(*exchange(seen), unseen, line_mask, row_table)
    *shares, summed = call(
        functools.partial(combine_kernel, depth, chips),
        "combine",
        [(2 * depth * share, width)] * coils + [image],
        [(2, depth, slabs, step, width)],
    )(*exchange(back), residual, coil_maps, warm_start, scaled_dual)
    shares = [
        values if k == 0 else spread_over("coil", coils, k)(values)
        for k, values in reversed(list(enumerate(shares)))
    ]
    shrunk = call(
        functools.partial(shrink_kernel, depth), "shrink", [(2 * depth * share, width)]
    )(*shares)
    shrunk = [
        shrunk if k == 0 else spread_over("coil", coils, k)(shrunk) for k in range(coils)
    ]
    return tuple(
        call(functools.partial(finish_kernel, depth), "finish", [image, (1, *image)])(
            *shrunk, summed
        )
    )


def solution(mesh):
    placed = (
        P("coil", None, "slab", None, None),
        P("coil", None, "slab", None, None),
        P(None, "slab", None, None),
        P("coil", None, None, "slab", None),
        P("coil", None, "slab", None, None),
        P(),
    )
    return jax.shard_map(
        per_device,
        mesh=mesh,
        in_specs=placed,
        out_specs=(P(None, "slab", None, None), P("coil", None, "slab", None, None)),
        check_vma=False,
    )
```

```python
import functools
import math

import jax
import jax.numpy as jnp
import numpy as np
from jax import lax
from jax.experimental import pallas as pl
from jax.experimental.pallas import tpu as pltpu
from jax.sharding import PartitionSpec as P

THRESHOLD = 0.15
ROOT_HALF = 0.7071067811865476
UNSEEN = 1e-20
F32 = jnp.float32
BF16 = jnp.bfloat16


def dft_table(length):
    index = np.arange(length)
    angles = (np.outer(index, index) % length) * (2.0 * math.pi / length)
    cosine = np.cos(angles) / math.sqrt(length)
    sine = np.sin(angles) / math.sqrt(length)
    whole = np.block([[cosine, sine], [-sine, cosine]]).astype(np.float32)
    high = whole.astype(jnp.bfloat16)
    low = (whole - high.astype(np.float32)).astype(jnp.bfloat16)
    return np.stack([high, low])


def halves(values):
    high = values.astype(BF16)
    return high, (values - high.astype(F32)).astype(BF16)


def contract(left, right, dims):
    return lax.dot_general(left, right, (dims, ((), ())), preferred_element_type=F32)


def rows_times_table(values, table_ref):
    high, low = halves(values)
    dims = ((1,), (1,))
    return (
        contract(high, table_ref[0], dims)
        + contract(high, table_ref[1], dims)
        + contract(low, table_ref[0], dims)
    )


def table_times_columns(table_ref, values):
    high, low = halves(values)
    dims = ((1,), (0,))
    return (
        contract(table_ref[0], high, dims)
        + contract(table_ref[1], high, dims)
        + contract(table_ref[0], low, dims)
    )


def fourier(real, imag, sign):
    count = len(real)
    if count == 1:
        return list(real), list(imag)
    if count % 2:
        out_real, out_imag = [], []
        for k in range(count):
            sum_real, sum_imag = real[0], imag[0]
            for n in range(1, count):
                angle = sign * 2.0 * math.pi * (k * n % count) / count
                c, s = math.cos(angle), math.sin(angle)
                sum_real = sum_real + (c * real[n] - s * imag[n])
                sum_imag = sum_imag + (c * imag[n] + s * real[n])
            out_real.append(sum_real)
            out_imag.append(sum_imag)
        return out_real, out_imag
    even_real, even_imag = fourier(real[0::2], imag[0::2], sign)
    odd_real, odd_imag = fourier(real[1::2], imag[1::2], sign)
    half = count // 2
    out_real, out_imag = [None] * count, [None] * count
    for k in range(half):
        x, y = odd_real[k], odd_imag[k]
        if k == 0:
            pass
        elif 4 * k == count:
            x, y = (-y, x) if sign > 0 else (y, -x)
        elif 8 * k == count:
            x, y = (x - sign * y) * ROOT_HALF, (y + sign * x) * ROOT_HALF
        elif 8 * k == 3 * count:
            x, y = (-x - sign * y) * ROOT_HALF, (sign * x - y) * ROOT_HALF
        else:
            angle = sign * 2.0 * math.pi * k / count
            c, s = math.cos(angle), math.sin(angle)
            x, y = c * x - s * y, c * y + s * x
        out_real[k], out_imag[k] = even_real[k] + x, even_imag[k] + y
        out_real[k + half], out_imag[k + half] = even_real[k] - x, even_imag[k] - y
    return out_real, out_imag


def total(values):
    return jnp.sum(values, axis=(0, 1), keepdims=True)


def row_tiles(count):
    step = 8 if count % 8 == 0 else count
    return [(start, step) for start in range(0, count, step)]


def placement():
    index = lax.axis_index("slab")
    return index >> 1, index & 1


def row_of(index, size):
    return pl.ds(pl.multiple_of(index * size, size), size)


def passed_on(chips, k):
    return 2 * k > chips


def routes(chips):
    far = [k for k in range(chips - 1, 0, -1) if passed_on(chips, k)]
    near = [k for k in range(1, chips) if not passed_on(chips, k)]
    return (
        [(k, 0) for k in far]
        + [(k, j) for k in near for j in range(2)]
        + [(0, 0), (0, 1)]
        + [(k, 1) for k in far[::-1]]
    )


def arrivals(chips, refs):
    chip, core = placement()
    return [
        (2 * (chip ^ k) + (core ^ j), ref) for (k, j), ref in zip(routes(chips), refs[: 2 * chips])
    ]


def departures(refs):
    chip, core = placement()
    return [
        (2 * (chip ^ k) + (core ^ j), ref.at[j]) for k, ref in enumerate(refs) for j in range(2)
    ]


def send_start_kernel(depth, start_hbm, maps_hbm, row_hbm, col_hbm, *refs):
    out_refs, (start_ref, maps_ref, row_table, col_table, work_ref, sems) = refs[:-6], refs[-6:]
    fetches = [
        pltpu.make_async_copy(source, target, sems.at[index])
        for index, (source, target) in enumerate(
            (
                (start_hbm, start_ref),
                (maps_hbm, maps_ref),
                (row_hbm, row_table),
                (col_hbm, col_table),
            )
        )
    ]
    for fetch in fetches:
        fetch.start()
    for fetch in fetches:
        fetch.wait()
    _, rows, width = out_refs[0].shape
    height = start_ref.shape[3]
    step = rows // (2 * depth)
    real, imag = start_ref[0, 0], start_ref[0, 1]
    map_real, map_imag = maps_ref[0, 0], maps_ref[0, 1]
    seen_real = (map_real * real - map_imag * imag).reshape(depth * height, width)
    seen_imag = (map_real * imag + map_imag * real).reshape(depth * height, width)
    along_y = rows_times_table(jnp.concatenate([seen_real, seen_imag], axis=1), row_table)
    columns = jnp.concatenate(
        [
            jnp.concatenate(
                [
                    along_y[z * height : (z + 1) * height, part * width : (part + 1) * width]
                    for z in range(depth)
                ],
                axis=1,
            )
            for part in range(2)
        ],
        axis=0,
    )
    spectrum = table_times_columns(col_table, columns)
    for part in range(2):
        for block in range(height // step):
            first = part * height + block * step
            work_ref[part, block] = spectrum[first : first + step]
    for block, out_ref in departures(out_refs):
        for part in range(2):
            for z in range(depth):
                out_ref[pl.ds((part * depth + z) * step, step), :] = work_ref[
                    part, block, :, z * width : (z + 1) * width
                ]


def sampled_residual_kernel(depth, chips, *refs):
    kspace_ref, mask_ref = refs[2 * chips : 2 * chips + 2]
    out_refs, work_ref = refs[2 * chips + 2 : -1], refs[-1]
    length, step = kspace_ref.shape[2], kspace_ref.shape[3]
    span = depth * step
    norm = 1.0 / math.sqrt(length)
    for slab, source in arrivals(chips, refs):
        for part in range(2):
            work_ref[part, row_of(slab, span), :] = source[0, pl.ds(part * span, span), :]
    for start, size in row_tiles(step):
        rows = [pl.ds(z * step + start, size) for z in range(length)]
        real = [work_ref[0, row, :] for row in rows]
        imag = [work_ref[1, row, :] for row in rows]
        real, imag = fourier(real, imag, -1.0)
        for z in range(length):
            weight = mask_ref[pl.ds(z, 1), :].astype(F32) * norm
            real[z] = weight * (kspace_ref[0, 0, z, pl.ds(start, size), :] - norm * real[z])
            imag[z] = weight * (kspace_ref[0, 1, z, pl.ds(start, size), :] - norm * imag[z])
        real, imag = fourier(real, imag, 1.0)
        for z, row in enumerate(rows):
            work_ref[0, row, :], work_ref[1, row, :] = real[z], imag[z]
    for slab, out_ref in departures(out_refs):
        for part in range(2):
            out_ref[pl.ds(part * span, span), :] = work_ref[part, row_of(slab, span), :]


def residual_kernel(depth, chips, *refs):
    (start_ref, dual_ref, consensus_ref, maps_ref, row_table, col_table) = refs[
        2 * chips : 2 * chips + 6
    ]
    residual_ref, unseen_ref = refs[2 * chips + 6 : 2 * chips + 8]
    send_refs, (work_ref, plane_ref) = refs[2 * chips + 8 : -2], refs[-2:]
    _, rows, width = refs[0].shape
    height = start_ref.shape[3]
    step = rows // (2 * depth)
    for block, source in arrivals(chips, refs):
        for part in range(2):
            for z in range(depth):
                work_ref[part, block, :, z * width : (z + 1) * width] = source[
                    0, pl.ds((part * depth + z) * step, step), :
                ]
    blocks = height // step
    columns = jnp.concatenate(
        [work_ref[part, block] for part in (1, 0) for block in range(blocks)], axis=0
    )
    along_x = table_times_columns(col_table, columns)
    rows = jnp.concatenate(
        [
            jnp.concatenate(
                [
                    along_x[part * height : (part + 1) * height, z * width : (z + 1) * width]
                    for part in range(2)
                ],
                axis=1,
            )
            for z in range(depth)
        ],
        axis=0,
    )
    image = rows_times_table(rows, row_table)
    unseen = jnp.zeros((8, width), F32)
    for z in range(depth):
        back_imag = image[z * height : (z + 1) * height, :width]
        back_real = image[z * height : (z + 1) * height, width:]
        map_real, map_imag = maps_ref[0, 0, z], maps_ref[0, 1, z]
        pull_real = consensus_ref[0, z] - dual_ref[0, 0, z] - start_ref[0, 0, z]
        pull_imag = consensus_ref[1, z] - dual_ref[0, 1, z] - start_ref[0, 1, z]
        real = map_real * back_real + map_imag * back_imag + pull_real
        imag = map_real * back_imag - map_imag * back_real + pull_imag
        residual_ref[0, z], residual_ref[1, z] = real, imag
        power = map_real * map_real + map_imag * map_imag
        hidden = jnp.where(power < UNSEEN, real * real + imag * imag, 0.0)
        unseen = unseen + jnp.sum(hidden.reshape(height // 8, 8, width), axis=0)
        for part, plane in enumerate(
            (map_real * real - map_imag * imag, map_real * imag + map_imag * real, power)
        ):
            for block in range(blocks):
                plane_ref[part, z, block] = plane[block * step : (block + 1) * step]
    unseen_ref[...] = unseen
    for block, send_ref in departures(send_refs):
        for part in range(3):
            for z in range(depth):
                send_ref[pl.ds((part * depth + z) * step, step), :] = plane_ref[part, z, block]


def normal_kernel(depth, chips, *refs):
    unseen_ref, mask_ref, row_table = refs[2 * chips : 2 * chips + 3]
    out_refs, (seen_ref, work_ref, held_ref) = refs[2 * chips + 3 : -3], refs[-3:]
    _, rows, width = refs[0].shape
    span = rows // 3
    step = span // depth
    length = depth * chips * 2
    norm = 1.0 / math.sqrt(length)
    for slab, source in arrivals(chips, refs):
        for part in range(3):
            seen_ref[part, row_of(slab, span), :] = source[0, pl.ds(part * span, span), :]

    def place(z, start):
        return z * step + start

    def weigh(z):
        return mask_ref[pl.ds(z, 1), :].astype(F32) * norm

    seen_real, seen_imag = seen_ref[0], seen_ref[1]
    along_y = rows_times_table(jnp.concatenate([seen_real, seen_imag], axis=1), row_table)
    work_ref[0], work_ref[1] = along_y[:, :width], along_y[:, width:]
    sampled = None
    for start, size in row_tiles(step):
        real = [work_ref[0, pl.ds(place(z, start), size), :] for z in range(length)]
        imag = [work_ref[1, pl.ds(place(z, start), size), :] for z in range(length)]
        real, imag = fourier(real, imag, -1.0)
        for z in range(length):
            weight = weigh(z)
            real[z], imag[z] = real[z] * weight, imag[z] * weight
            held_ref[0, pl.ds(place(z, start), size), :] = real[z]
            held_ref[1, pl.ds(place(z, start), size), :] = imag[z]
            term = real[z] * real[z] + imag[z] * imag[z]
            sampled = term if sampled is None else sampled + term
        real, imag = fourier(real, imag, 1.0)
        for z in range(length):
            work_ref[0, pl.ds(place(z, start), size), :] = real[z] * norm
            work_ref[1, pl.ds(place(z, start), size), :] = imag[z] * norm
    image = rows_times_table(jnp.concatenate([work_ref[1], work_ref[0]], axis=1), row_table)
    back_real, back_imag = image[:, width:], image[:, :width]
    work_ref[0], work_ref[1] = back_real, back_imag
    for slab, out_ref in departures(out_refs):
        for part in range(2):
            out_ref[pl.ds(part * span, span), :] = work_ref[part, row_of(slab, span), :]
    power = seen_ref[2]
    inverse = jnp.where(power < UNSEEN, 0.0, 1.0 / jnp.maximum(power, UNSEEN))
    first = total((seen_real * seen_real + seen_imag * seen_imag) * inverse)
    sampled = total(sampled)
    slope = jnp.where(first > 0.0, sampled / jnp.where(first > 0.0, first, 1.0), 0.0)
    rest_real = power * back_real - slope * seen_real
    rest_imag = power * back_imag - slope * seen_imag
    spread = total((rest_real * rest_real + rest_imag * rest_imag) * inverse)
    along_y = rows_times_table(jnp.concatenate([rest_real, rest_imag], axis=1), row_table)
    work_ref[0], work_ref[1] = along_y[:, :width], along_y[:, width:]
    energy, cross = None, None
    for start, size in row_tiles(step):
        real = [work_ref[0, pl.ds(place(z, start), size), :] for z in range(length)]
        imag = [work_ref[1, pl.ds(place(z, start), size), :] for z in range(length)]
        real, imag = fourier(real, imag, -1.0)
        for z in range(length):
            weight = weigh(z)
            real[z], imag[z] = real[z] * weight, imag[z] * weight
            term = real[z] * real[z] + imag[z] * imag[z]
            other_term = (
                real[z] * held_ref[0, pl.ds(place(z, start), size), :]
                + imag[z] * held_ref[1, pl.ds(place(z, start), size), :]
            )
            energy = term if energy is None else energy + term
            cross = other_term if cross is None else cross + other_term
    line = lax.broadcasted_iota(jnp.int32, (8, width), 0)
    sums = jnp.zeros((8, width), F32)
    shares = (first, sampled, spread, total(energy), total(cross), total(unseen_ref[...]))
    for index, share in enumerate(shares):
        sums = jnp.where(line == index, share, sums)
    for out_ref in out_refs:
        for j in range(2):
            out_ref[j, pl.ds(2 * span, 8), :] = sums


def combine_kernel(depth, chips, *refs):
    residual_ref, maps_ref, start_ref, dual_ref = refs[2 * chips : 2 * chips + 4]
    send_refs, sum_ref, back_ref = refs[2 * chips + 4 : -2], refs[-2], refs[-1]
    _, rows, width = refs[0].shape
    span = (rows - 8) // 2
    step = span // depth
    height = start_ref.shape[3]
    parts = len(send_refs)
    share = height // parts
    sources = arrivals(chips, refs)
    sums = [source[0, pl.ds(2 * span, 8), :] for _, source in sources]
    added = functools.reduce(lambda a, b: a + b, sums)
    unseen = added[5:6]
    norm_first = added[0:1] + unseen
    sampled = added[1:2]
    slope = sampled / norm_first
    spread = slope * slope * unseen
    energy = jnp.zeros_like(unseen)
    for shares in sums:
        own, own_sampled = shares[0:1], shares[1:2]
        own_slope = jnp.where(own > 0.0, own_sampled / jnp.where(own > 0.0, own, 1.0), 0.0)
        shift = slope - own_slope
        spread = spread + shares[2:3] + shift * shift * own
        energy = energy + shares[3:4] - 2.0 * shift * shares[4:5] + shift * shift * own_sampled
    alpha_first = norm_first / (norm_first + sampled)
    beta = alpha_first * alpha_first * spread / norm_first
    curve = spread + energy - alpha_first * spread * spread / norm_first
    alpha_second = jnp.where(spread > 0.0, spread / jnp.where(spread > 0.0, curve, 1.0), 0.0)
    along_residual = alpha_first + alpha_second * (alpha_first * slope + beta)
    along_back = -alpha_first * alpha_second
    for block, source in sources:
        for part in range(2):
            for z in range(depth):
                back_ref[part, z, block] = source[0, pl.ds(part * span + z * step, step), :]
    for block in range(height // step):
        window = pl.ds(block * step, step)
        for z in range(depth):
            back_real = back_ref[0, z, block] * along_back
            back_imag = back_ref[1, z, block] * along_back
            map_real, map_imag = maps_ref[0, 0, z, window, :], maps_ref[0, 1, z, window, :]
            moves = (
                map_real * back_real + map_imag * back_imag,
                map_real * back_imag - map_imag * back_real,
            )
            for part in range(2):
                sum_ref[part, z, window, :] = (
                    start_ref[0, part, z, window, :]
                    + dual_ref[0, part, z, window, :]
                    + along_residual * residual_ref[part, z, window, :]
                    + moves[part]
                )
    coil = lax.axis_index("coil")
    for k in range(parts):
        window = row_of(coil ^ k, share)
        for part in range(2):
            for z in range(depth):
                send_refs[k][pl.ds((part * depth + z) * share, share), :] = sum_ref[
                    part, z, window, :
                ]


def shrink_kernel(depth, *refs):
    all_refs, out_ref = refs[:-1], refs[-1]
    coils = len(all_refs)
    rows, width = out_ref.shape
    share = rows // (2 * depth)
    line = lax.broadcasted_iota(jnp.int32, (share, width), 0) % 2
    lane = lax.broadcasted_iota(jnp.int32, (share, width), 1) % 2
    low = (line == 0) & (lane == 0)

    def along_lines(cells):
        near = jnp.where(
            line == 0, pltpu.roll(cells, share - 1, 0), pltpu.roll(cells, 1, 0) - 2.0 * cells
        )
        return (cells + near) * ROOT_HALF

    def along_lanes(cells):
        near = jnp.where(
            lane == 0, pltpu.roll(cells, width - 1, 1), pltpu.roll(cells, 1, 1) - 2.0 * cells
        )
        return (cells + near) * ROOT_HALF

    def mean(part, z):
        window = pl.ds((part * depth + z) * share, share)
        return functools.reduce(lambda a, b: a + b, [ref[window, :] for ref in all_refs]) * (
            1.0 / coils
        )

    for z in range(0, depth, 2):
        bands = []
        for part in range(2):
            first, second = mean(part, z), mean(part, z + 1)
            bands.append(
                [
                    along_lanes(along_lines(band))
                    for band in ((first + second) * ROOT_HALF, (first - second) * ROOT_HALF)
                ]
            )
        kept = [[], []]
        for level in range(2):
            real, imag = bands[0][level], bands[1][level]
            size = jnp.sqrt(real * real + imag * imag)
            factor = jnp.maximum(size - THRESHOLD, 0.0) / jnp.maximum(size, THRESHOLD)
            if level == 0:
                factor = jnp.where(low, 1.0, factor)
            kept[0].append(along_lines(along_lanes(real * factor)))
            kept[1].append(along_lines(along_lanes(imag * factor)))
        for part in range(2):
            base, detail = kept[part]
            out_ref[pl.ds((part * depth + z) * share, share), :] = (base + detail) * ROOT_HALF
            out_ref[pl.ds((part * depth + z + 1) * share, share), :] = (base - detail) * ROOT_HALF


def finish_kernel(depth, *refs):
    parts = len(refs) - 3
    sum_ref, consensus_ref, dual_ref = refs[parts:]
    share = refs[0].shape[0] // (2 * depth)
    coil = lax.axis_index("coil")
    for k in range(parts):
        window = row_of(coil ^ k, share)
        for part in range(2):
            for z in range(depth):
                cells = refs[k][pl.ds((part * depth + z) * share, share), :]
                consensus_ref[part, z, window, :] = cells
                dual_ref[0, part, z, window, :] = sum_ref[part, z, window, :] - cells


def call(kernel, name, outs, scratch=(), fetched=False):
    in_vmem = pl.BlockSpec(memory_space=pltpu.VMEM)
    left = pl.BlockSpec(memory_space=pltpu.HBM)
    shapes = [jax.ShapeDtypeStruct(shape, F32) for shape in outs]

    def run(*operands):
        return pl.pallas_call(
            kernel,
            name=name,
            out_shape=shapes if len(shapes) > 1 else shapes[0],
            in_specs=[left if fetched else in_vmem] * len(operands),
            out_specs=[in_vmem] * len(shapes) if len(shapes) > 1 else in_vmem,
            scratch_shapes=[pltpu.VMEM(s, F32) if isinstance(s, tuple) else s for s in scratch],
            compiler_params=pltpu.CompilerParams(vmem_limit_bytes=32 << 20),
        )(*operands)

    return run


def spread_over(axis, size, mask):
    return lambda values: lax.ppermute(values, axis, [(i, i ^ mask) for i in range(size)])


def per_device(warm_start, scaled_dual, consensus, kspace, coil_maps, line_mask):
    depth, height, width = warm_start.shape[2:]
    slabs, coils = lax.axis_size("slab"), lax.axis_size("coil")
    chips = slabs // 2
    step = height // slabs
    span = depth * step
    share = height // coils
    row_table = jnp.asarray(dft_table(width))
    col_table = row_table if height == width else jnp.asarray(dft_table(height))
    tables = (row_table, col_table)
    table_shapes = [pltpu.VMEM(table.shape, BF16) for table in tables]
    image = (2, depth, height, width)

    def exchange(pieces):
        landed = {(0, 0): pieces[0], (0, 1): spread_over("slab", slabs, 1)(pieces[0][1:2])}
        for k in range(1, chips):
            if passed_on(chips, k):
                landed[k, 0] = spread_over("slab", slabs, 2 * k)(pieces[k])
                landed[k, 1] = spread_over("slab", slabs, 1)(landed[k, 0][1:2])
                continue
            for j in range(2):
                half, _ = lax.optimization_barrier((pieces[k][j : j + 1], landed[0, 1]))
                landed[k, j] = spread_over("slab", slabs, 2 * k + j)(half)
        return [landed[route] for route in routes(chips)]

    piece = (2, 2 * span, width)
    seen = call(
        functools.partial(send_start_kernel, depth),
        "send_start",
        [piece] * chips,
        [
            warm_start.shape,
            coil_maps.shape,
            *table_shapes,
            (2, slabs, step, depth * width),
            pltpu.SemaphoreType.DMA((4,)),
        ],
        fetched=True,
    )(
        *(
            pltpu.with_memory_space_constraint(operand, pltpu.HBM)
            for operand in (warm_start, coil_maps, *tables)
        )
    )
    back = call(
        functools.partial(sampled_residual_kernel, depth, chips),
        "sampled_residual",
        [piece] * chips,
        [(2, slabs * span, width)],
    )(*exchange(seen), kspace, line_mask)
    residual, unseen, *seen = call(
        functools.partial(residual_kernel, depth, chips),
        "residual",
        [image, (8, width)] + [(2, 3 * span, width)] * chips,
        [(2, slabs, step, depth * width), (3, depth, slabs, step, width)],
    )(*exchange(back), warm_start, scaled_dual, consensus, coil_maps, *tables)
    back = call(
        functools.partial(normal_kernel, depth, chips),
        "normal",
        [(2, 2 * span + 8, width)] * chips,
        [(parts, slabs * span, width) for parts in (3, 2, 2)],
    )(*exchange(seen), unseen, line_mask, row_table)
    *shares, summed = call(
        functools.partial(combine_kernel, depth, chips),
        "combine",
        [(2 * depth * share, width)] * coils + [image],
        [(2, depth, slabs, step, width)],
    )(*exchange(back), residual, coil_maps, warm_start, scaled_dual)
    shares = [
        values if k == 0 else spread_over("coil", coils, k)(values)
        for k, values in enumerate(shares)
    ]
    shrunk = call(
        functools.partial(shrink_kernel, depth), "shrink", [(2 * depth * share, width)]
    )(*shares)
    shrunk = [
        shrunk if k == 0 else spread_over("coil", coils, k)(shrunk) for k in range(coils)
    ]
    return tuple(
        call(functools.partial(finish_kernel, depth), "finish", [image, (1, *image)])(
            *shrunk, summed
        )
    )


def solution(mesh):
    placed = (
        P("coil", None, "slab", None, None),
        P("coil", None, "slab", None, None),
        P(None, "slab", None, None),
        P("coil", None, None, "slab", None),
        P("coil", None, "slab", None, None),
        P(),
    )
    return jax.shard_map(
        per_device,
        mesh=mesh,
        in_specs=placed,
        out_specs=(P(None, "slab", None, None), P("coil", None, "slab", None, None)),
        check_vma=False,
    )
```

```python
import functools
import math

import jax
import jax.numpy as jnp
import numpy as np
from jax import lax
from jax.experimental import pallas as pl
from jax.experimental.pallas import tpu as pltpu
from jax.sharding import PartitionSpec as P

THRESHOLD = 0.15
ROOT_HALF = 0.7071067811865476
UNSEEN = 1e-20
F32 = jnp.float32
BF16 = jnp.bfloat16


def dft_table(length):
    index = np.arange(length)
    angles = (np.outer(index, index) % length) * (2.0 * math.pi / length)
    cosine = np.cos(angles) / math.sqrt(length)
    sine = np.sin(angles) / math.sqrt(length)
    whole = np.block([[cosine, sine], [-sine, cosine]]).astype(np.float32)
    high = whole.astype(jnp.bfloat16)
    low = (whole - high.astype(np.float32)).astype(jnp.bfloat16)
    return np.stack([high, low])


def halves(values):
    high = values.astype(BF16)
    return high, (values - high.astype(F32)).astype(BF16)


def contract(left, right, dims):
    return lax.dot_general(left, right, (dims, ((), ())), preferred_element_type=F32)


def rows_times_table(values, table_ref):
    high, low = halves(values)
    dims = ((1,), (1,))
    return (
        contract(high, table_ref[0], dims)
        + contract(high, table_ref[1], dims)
        + contract(low, table_ref[0], dims)
    )


def table_times_columns(table_ref, values):
    high, low = halves(values)
    dims = ((1,), (0,))
    return (
        contract(table_ref[0], high, dims)
        + contract(table_ref[1], high, dims)
        + contract(table_ref[0], low, dims)
    )


def fourier(real, imag, sign):
    count = len(real)
    if count == 1:
        return list(real), list(imag)
    if count % 2:
        out_real, out_imag = [], []
        for k in range(count):
            sum_real, sum_imag = real[0], imag[0]
            for n in range(1, count):
                angle = sign * 2.0 * math.pi * (k * n % count) / count
                c, s = math.cos(angle), math.sin(angle)
                sum_real = sum_real + (c * real[n] - s * imag[n])
                sum_imag = sum_imag + (c * imag[n] + s * real[n])
            out_real.append(sum_real)
            out_imag.append(sum_imag)
        return out_real, out_imag
    even_real, even_imag = fourier(real[0::2], imag[0::2], sign)
    odd_real, odd_imag = fourier(real[1::2], imag[1::2], sign)
    half = count // 2
    out_real, out_imag = [None] * count, [None] * count
    for k in range(half):
        x, y = odd_real[k], odd_imag[k]
        if k == 0:
            pass
        elif 4 * k == count:
            x, y = (-y, x) if sign > 0 else (y, -x)
        elif 8 * k == count:
            x, y = (x - sign * y) * ROOT_HALF, (y + sign * x) * ROOT_HALF
        elif 8 * k == 3 * count:
            x, y = (-x - sign * y) * ROOT_HALF, (sign * x - y) * ROOT_HALF
        else:
            angle = sign * 2.0 * math.pi * k / count
            c, s = math.cos(angle), math.sin(angle)
            x, y = c * x - s * y, c * y + s * x
        out_real[k], out_imag[k] = even_real[k] + x, even_imag[k] + y
        out_real[k + half], out_imag[k + half] = even_real[k] - x, even_imag[k] - y
    return out_real, out_imag


def total(values):
    return jnp.sum(values, axis=(0, 1), keepdims=True)


def row_tiles(count):
    step = 8 if count % 8 == 0 else count
    return [(start, step) for start in range(0, count, step)]


def placement():
    index = lax.axis_index("slab")
    return index >> 1, index & 1


def row_of(index, size):
    return pl.ds(pl.multiple_of(index * size, size), size)


def passed_on(chips, k):
    return 2 * k > chips


def routes(chips):
    far = [k for k in range(chips - 1, 0, -1) if passed_on(chips, k)]
    near = [k for k in range(1, chips) if not passed_on(chips, k)]
    return (
        [(k, 0) for k in far]
        + [(k, j) for k in near for j in range(2)]
        + [(0, 0), (0, 1)]
        + [(k, 1) for k in far[::-1]]
    )


def arrivals(chips, refs):
    chip, core = placement()
    return [
        (2 * (chip ^ k) + (core ^ j), ref) for (k, j), ref in zip(routes(chips), refs[: 2 * chips])
    ]


def departures(refs):
    chip, core = placement()
    return [
        (2 * (chip ^ k) + (core ^ j), ref.at[j]) for k, ref in enumerate(refs) for j in range(2)
    ]


def send_start_kernel(depth, given, *refs):
    sources, out_refs, held = refs[:given], refs[given : -given - 2], refs[-given - 2 : -2]
    work_ref, sems = refs[-2:]
    fetches = [
        pltpu.make_async_copy(source, target, sems.at[index])
        for index, (source, target) in enumerate(zip(sources, held))
    ]
    for fetch in fetches:
        fetch.start()
    for fetch in fetches[:2]:
        fetch.wait()
    start_ref, maps_ref, row_table, col_table = held[0], held[1], held[2], held[-1]
    _, rows, width = out_refs[0].shape
    height = start_ref.shape[3]
    step = rows // (2 * depth)
    real, imag = start_ref[0, 0], start_ref[0, 1]
    map_real, map_imag = maps_ref[0, 0], maps_ref[0, 1]
    seen_real = (map_real * real - map_imag * imag).reshape(depth * height, width)
    seen_imag = (map_real * imag + map_imag * real).reshape(depth * height, width)
    for fetch in fetches[2:]:
        fetch.wait()
    along_y = rows_times_table(jnp.concatenate([seen_real, seen_imag], axis=1), row_table)
    columns = jnp.concatenate(
        [
            jnp.concatenate(
                [
                    along_y[z * height : (z + 1) * height, part * width : (part + 1) * width]
                    for z in range(depth)
                ],
                axis=1,
            )
            for part in range(2)
        ],
        axis=0,
    )
    spectrum = table_times_columns(col_table, columns)
    for part in range(2):
        for block in range(height // step):
            first = part * height + block * step
            work_ref[part, block] = spectrum[first : first + step]
    for block, out_ref in departures(out_refs):
        for part in range(2):
            for z in range(depth):
                out_ref[pl.ds((part * depth + z) * step, step), :] = work_ref[
                    part, block, :, z * width : (z + 1) * width
                ]


def sampled_residual_kernel(depth, chips, *refs):
    kspace_ref, mask_ref = refs[2 * chips : 2 * chips + 2]
    out_refs, work_ref = refs[2 * chips + 2 : -1], refs[-1]
    length, step = kspace_ref.shape[2], kspace_ref.shape[3]
    span = depth * step
    norm = 1.0 / math.sqrt(length)
    for slab, source in arrivals(chips, refs):
        for part in range(2):
            work_ref[part, row_of(slab, span), :] = source[0, pl.ds(part * span, span), :]
    for start, size in row_tiles(step):
        rows = [pl.ds(z * step + start, size) for z in range(length)]
        real = [work_ref[0, row, :] for row in rows]
        imag = [work_ref[1, row, :] for row in rows]
        real, imag = fourier(real, imag, -1.0)
        for z in range(length):
            weight = mask_ref[pl.ds(z, 1), :].astype(F32) * norm
            real[z] = weight * (kspace_ref[0, 0, z, pl.ds(start, size), :] - norm * real[z])
            imag[z] = weight * (kspace_ref[0, 1, z, pl.ds(start, size), :] - norm * imag[z])
        real, imag = fourier(real, imag, 1.0)
        for z, row in enumerate(rows):
            work_ref[0, row, :], work_ref[1, row, :] = real[z], imag[z]
    for slab, out_ref in departures(out_refs):
        for part in range(2):
            out_ref[pl.ds(part * span, span), :] = work_ref[part, row_of(slab, span), :]


def residual_kernel(depth, chips, *refs):
    (start_ref, dual_ref, consensus_ref, maps_ref, row_table, col_table) = refs[
        2 * chips : 2 * chips + 6
    ]
    residual_ref, unseen_ref = refs[2 * chips + 6 : 2 * chips + 8]
    send_refs, (work_ref, plane_ref) = refs[2 * chips + 8 : -2], refs[-2:]
    _, rows, width = refs[0].shape
    height = start_ref.shape[3]
    step = rows // (2 * depth)
    for block, source in arrivals(chips, refs):
        for part in range(2):
            for z in range(depth):
                work_ref[part, block, :, z * width : (z + 1) * width] = source[
                    0, pl.ds((part * depth + z) * step, step), :
                ]
    blocks = height // step
    columns = jnp.concatenate(
        [work_ref[part, block] for part in (1, 0) for block in range(blocks)], axis=0
    )
    along_x = table_times_columns(col_table, columns)
    rows = jnp.concatenate(
        [
            jnp.concatenate(
                [
                    along_x[part * height : (part + 1) * height, z * width : (z + 1) * width]
                    for part in range(2)
                ],
                axis=1,
            )
            for z in range(depth)
        ],
        axis=0,
    )
    image = rows_times_table(rows, row_table)
    unseen = jnp.zeros((8, width), F32)
    for z in range(depth):
        back_imag = image[z * height : (z + 1) * height, :width]
        back_real = image[z * height : (z + 1) * height, width:]
        map_real, map_imag = maps_ref[0, 0, z], maps_ref[0, 1, z]
        pull_real = consensus_ref[0, z] - dual_ref[0, 0, z] - start_ref[0, 0, z]
        pull_imag = consensus_ref[1, z] - dual_ref[0, 1, z] - start_ref[0, 1, z]
        real = map_real * back_real + map_imag * back_imag + pull_real
        imag = map_real * back_imag - map_imag * back_real + pull_imag
        residual_ref[0, z], residual_ref[1, z] = real, imag
        power = map_real * map_real + map_imag * map_imag
        hidden = jnp.where(power < UNSEEN, real * real + imag * imag, 0.0)
        unseen = unseen + jnp.sum(hidden.reshape(height // 8, 8, width), axis=0)
        for part, plane in enumerate(
            (map_real * real - map_imag * imag, map_real * imag + map_imag * real, power)
        ):
            for block in range(blocks):
                plane_ref[part, z, block] = plane[block * step : (block + 1) * step]
    unseen_ref[...] = unseen
    for block, send_ref in departures(send_refs):
        for part in range(3):
            for z in range(depth):
                send_ref[pl.ds((part * depth + z) * step, step), :] = plane_ref[part, z, block]


def normal_kernel(depth, chips, *refs):
    unseen_ref, mask_ref, row_table = refs[2 * chips : 2 * chips + 3]
    out_refs, (seen_ref, work_ref, held_ref) = refs[2 * chips + 3 : -3], refs[-3:]
    _, rows, width = refs[0].shape
    span = rows // 3
    step = span // depth
    length = depth * chips * 2
    norm = 1.0 / math.sqrt(length)
    for slab, source in arrivals(chips, refs):
        for part in range(3):
            seen_ref[part, row_of(slab, span), :] = source[0, pl.ds(part * span, span), :]

    def place(z, start):
        return z * step + start

    def weigh(z):
        return mask_ref[pl.ds(z, 1), :].astype(F32) * norm

    seen_real, seen_imag = seen_ref[0], seen_ref[1]
    along_y = rows_times_table(jnp.concatenate([seen_real, seen_imag], axis=1), row_table)
    work_ref[0], work_ref[1] = along_y[:, :width], along_y[:, width:]
    sampled = None
    for start, size in row_tiles(step):
        real = [work_ref[0, pl.ds(place(z, start), size), :] for z in range(length)]
        imag = [work_ref[1, pl.ds(place(z, start), size), :] for z in range(length)]
        real, imag = fourier(real, imag, -1.0)
        for z in range(length):
            weight = weigh(z)
            real[z], imag[z] = real[z] * weight, imag[z] * weight
            held_ref[0, pl.ds(place(z, start), size), :] = real[z]
            held_ref[1, pl.ds(place(z, start), size), :] = imag[z]
            term = real[z] * real[z] + imag[z] * imag[z]
            sampled = term if sampled is None else sampled + term
        real, imag = fourier(real, imag, 1.0)
        for z in range(length):
            work_ref[0, pl.ds(place(z, start), size), :] = real[z] * norm
            work_ref[1, pl.ds(place(z, start), size), :] = imag[z] * norm
    image = rows_times_table(jnp.concatenate([work_ref[1], work_ref[0]], axis=1), row_table)
    back_real, back_imag = image[:, width:], image[:, :width]
    work_ref[0], work_ref[1] = back_real, back_imag
    for slab, out_ref in departures(out_refs):
        for part in range(2):
            out_ref[pl.ds(part * span, span), :] = work_ref[part, row_of(slab, span), :]
    power = seen_ref[2]
    inverse = jnp.where(power < UNSEEN, 0.0, 1.0 / jnp.maximum(power, UNSEEN))
    first = total((seen_real * seen_real + seen_imag * seen_imag) * inverse)
    sampled = total(sampled)
    slope = jnp.where(first > 0.0, sampled / jnp.where(first > 0.0, first, 1.0), 0.0)
    rest_real = power * back_real - slope * seen_real
    rest_imag = power * back_imag - slope * seen_imag
    spread = total((rest_real * rest_real + rest_imag * rest_imag) * inverse)
    along_y = rows_times_table(jnp.concatenate([rest_real, rest_imag], axis=1), row_table)
    work_ref[0], work_ref[1] = along_y[:, :width], along_y[:, width:]
    energy, cross = None, None
    for start, size in row_tiles(step):
        real = [work_ref[0, pl.ds(place(z, start), size), :] for z in range(length)]
        imag = [work_ref[1, pl.ds(place(z, start), size), :] for z in range(length)]
        real, imag = fourier(real, imag, -1.0)
        for z in range(length):
            weight = weigh(z)
            real[z], imag[z] = real[z] * weight, imag[z] * weight
            term = real[z] * real[z] + imag[z] * imag[z]
            other_term = (
                real[z] * held_ref[0, pl.ds(place(z, start), size), :]
                + imag[z] * held_ref[1, pl.ds(place(z, start), size), :]
            )
            energy = term if energy is None else energy + term
            cross = other_term if cross is None else cross + other_term
    line = lax.broadcasted_iota(jnp.int32, (8, width), 0)
    sums = jnp.zeros((8, width), F32)
    shares = (first, sampled, spread, total(energy), total(cross), total(unseen_ref[...]))
    for index, share in enumerate(shares):
        sums = jnp.where(line == index, share, sums)
    for out_ref in out_refs:
        for j in range(2):
            out_ref[j, pl.ds(2 * span, 8), :] = sums


def combine_kernel(depth, chips, *refs):
    residual_ref, maps_ref, start_ref, dual_ref = refs[2 * chips : 2 * chips + 4]
    send_refs, sum_ref, back_ref = refs[2 * chips + 4 : -2], refs[-2], refs[-1]
    _, rows, width = refs[0].shape
    span = (rows - 8) // 2
    step = span // depth
    height = start_ref.shape[3]
    parts = len(send_refs)
    share = height // parts
    sources = arrivals(chips, refs)
    sums = [source[0, pl.ds(2 * span, 8), :] for _, source in sources]
    added = functools.reduce(lambda a, b: a + b, sums)
    unseen = added[5:6]
    norm_first = added[0:1] + unseen
    sampled = added[1:2]
    slope = sampled / norm_first
    spread = slope * slope * unseen
    energy = jnp.zeros_like(unseen)
    for shares in sums:
        own, own_sampled = shares[0:1], shares[1:2]
        own_slope = jnp.where(own > 0.0, own_sampled / jnp.where(own > 0.0, own, 1.0), 0.0)
        shift = slope - own_slope
        spread = spread + shares[2:3] + shift * shift * own
        energy = energy + shares[3:4] - 2.0 * shift * shares[4:5] + shift * shift * own_sampled
    alpha_first = norm_first / (norm_first + sampled)
    beta = alpha_first * alpha_first * spread / norm_first
    curve = spread + energy - alpha_first * spread * spread / norm_first
    alpha_second = jnp.where(spread > 0.0, spread / jnp.where(spread > 0.0, curve, 1.0), 0.0)
    along_residual = alpha_first + alpha_second * (alpha_first * slope + beta)
    along_back = -alpha_first * alpha_second
    for block, source in sources:
        for part in range(2):
            for z in range(depth):
                back_ref[part, z, block] = source[0, pl.ds(part * span + z * step, step), :]
    for block in range(height // step):
        window = pl.ds(block * step, step)
        for z in range(depth):
            back_real = back_ref[0, z, block] * along_back
            back_imag = back_ref[1, z, block] * along_back
            map_real, map_imag = maps_ref[0, 0, z, window, :], maps_ref[0, 1, z, window, :]
            moves = (
                map_real * back_real + map_imag * back_imag,
                map_real * back_imag - map_imag * back_real,
            )
            for part in range(2):
                sum_ref[part, z, window, :] = (
                    start_ref[0, part, z, window, :]
                    + dual_ref[0, part, z, window, :]
                    + along_residual * residual_ref[part, z, window, :]
                    + moves[part]
                )
    coil = lax.axis_index("coil")
    for k in range(parts):
        window = row_of(coil ^ k, share)
        for part in range(2):
            for z in range(depth):
                send_refs[k][pl.ds((part * depth + z) * share, share), :] = sum_ref[
                    part, z, window, :
                ]


def shrink_kernel(depth, *refs):
    all_refs, out_ref = refs[:-1], refs[-1]
    coils = len(all_refs)
    rows, width = out_ref.shape
    share = rows // (2 * depth)
    line = lax.broadcasted_iota(jnp.int32, (share, width), 0) % 2
    lane = lax.broadcasted_iota(jnp.int32, (share, width), 1) % 2
    low = (line == 0) & (lane == 0)

    def along_lines(cells):
        near = jnp.where(
            line == 0, pltpu.roll(cells, share - 1, 0), pltpu.roll(cells, 1, 0) - 2.0 * cells
        )
        return (cells + near) * ROOT_HALF

    def along_lanes(cells):
        near = jnp.where(
            lane == 0, pltpu.roll(cells, width - 1, 1), pltpu.roll(cells, 1, 1) - 2.0 * cells
        )
        return (cells + near) * ROOT_HALF

    def mean(part, z):
        window = pl.ds((part * depth + z) * share, share)
        return functools.reduce(lambda a, b: a + b, [ref[window, :] for ref in all_refs]) * (
            1.0 / coils
        )

    for z in range(0, depth, 2):
        bands = []
        for part in range(2):
            first, second = mean(part, z), mean(part, z + 1)
            bands.append(
                [
                    along_lanes(along_lines(band))
                    for band in ((first + second) * ROOT_HALF, (first - second) * ROOT_HALF)
                ]
            )
        kept = [[], []]
        for level in range(2):
            real, imag = bands[0][level], bands[1][level]
            size = jnp.sqrt(real * real + imag * imag)
            factor = jnp.maximum(size - THRESHOLD, 0.0) / jnp.maximum(size, THRESHOLD)
            if level == 0:
                factor = jnp.where(low, 1.0, factor)
            kept[0].append(along_lines(along_lanes(real * factor)))
            kept[1].append(along_lines(along_lanes(imag * factor)))
        for part in range(2):
            base, detail = kept[part]
            out_ref[pl.ds((part * depth + z) * share, share), :] = (base + detail) * ROOT_HALF
            out_ref[pl.ds((part * depth + z + 1) * share, share), :] = (base - detail) * ROOT_HALF


def finish_kernel(depth, *refs):
    parts = len(refs) - 3
    sum_ref, consensus_ref, dual_ref = refs[parts:]
    share = refs[0].shape[0] // (2 * depth)
    coil = lax.axis_index("coil")
    for k in range(parts):
        window = row_of(coil ^ k, share)
        for part in range(2):
            for z in range(depth):
                cells = refs[k][pl.ds((part * depth + z) * share, share), :]
                consensus_ref[part, z, window, :] = cells
                dual_ref[0, part, z, window, :] = sum_ref[part, z, window, :] - cells


def call(kernel, name, outs, scratch=(), fetched=False):
    in_vmem = pl.BlockSpec(memory_space=pltpu.VMEM)
    left = pl.BlockSpec(memory_space=pltpu.HBM)
    shapes = [jax.ShapeDtypeStruct(shape, F32) for shape in outs]

    def run(*operands):
        return pl.pallas_call(
            kernel,
            name=name,
            out_shape=shapes if len(shapes) > 1 else shapes[0],
            in_specs=[left if fetched else in_vmem] * len(operands),
            out_specs=[in_vmem] * len(shapes) if len(shapes) > 1 else in_vmem,
            scratch_shapes=[pltpu.VMEM(s, F32) if isinstance(s, tuple) else s for s in scratch],
            compiler_params=pltpu.CompilerParams(vmem_limit_bytes=32 << 20),
        )(*operands)

    return run


def spread_over(axis, size, mask):
    return lambda values: lax.ppermute(values, axis, [(i, i ^ mask) for i in range(size)])


def per_device(warm_start, scaled_dual, consensus, kspace, coil_maps, line_mask):
    depth, height, width = warm_start.shape[2:]
    slabs, coils = lax.axis_size("slab"), lax.axis_size("coil")
    chips = slabs // 2
    step = height // slabs
    span = depth * step
    share = height // coils
    row_table = jnp.asarray(dft_table(width))
    col_table = row_table if height == width else jnp.asarray(dft_table(height))
    tables = (row_table, col_table)
    image = (2, depth, height, width)

    def exchange(pieces):
        landed = {(0, 0): pieces[0], (0, 1): spread_over("slab", slabs, 1)(pieces[0][1:2])}
        for k in range(1, chips):
            if passed_on(chips, k):
                landed[k, 0] = spread_over("slab", slabs, 2 * k)(pieces[k])
                landed[k, 1] = spread_over("slab", slabs, 1)(landed[k, 0][1:2])
                continue
            for j in range(2):
                half, _ = lax.optimization_barrier((pieces[k][j : j + 1], landed[0, 1]))
                landed[k, j] = spread_over("slab", slabs, 2 * k + j)(half)
        return [landed[route] for route in routes(chips)]

    piece = (2, 2 * span, width)
    own_tables = tables[:1] if row_table is col_table else tables
    fetched = (warm_start, coil_maps, *own_tables)
    seen = call(
        functools.partial(send_start_kernel, depth, len(fetched)),
        "send_start",
        [piece] * chips,
        [
            warm_start.shape,
            coil_maps.shape,
            *(pltpu.VMEM(table.shape, BF16) for table in own_tables),
            (2, slabs, step, depth * width),
            pltpu.SemaphoreType.DMA((len(fetched),)),
        ],
        fetched=True,
    )(*(pltpu.with_memory_space_constraint(operand, pltpu.HBM) for operand in fetched))
    back = call(
        functools.partial(sampled_residual_kernel, depth, chips),
        "sampled_residual",
        [piece] * chips,
        [(2, slabs * span, width)],
    )(*exchange(seen), kspace, line_mask)
    residual, unseen, *seen = call(
        functools.partial(residual_kernel, depth, chips),
        "residual",
        [image, (8, width)] + [(2, 3 * span, width)] * chips,
        [(2, slabs, step, depth * width), (3, depth, slabs, step, width)],
    )(*exchange(back), warm_start, scaled_dual, consensus, coil_maps, *tables)
    back = call(
        functools.partial(normal_kernel, depth, chips),
        "normal",
        [(2, 2 * span + 8, width)] * chips,
        [(parts, slabs * span, width) for parts in (3, 2, 2)],
    )(*exchange(seen), unseen, line_mask, row_table)
    *shares, summed = call(
        functools.partial(combine_kernel, depth, chips),
        "combine",
        [(2 * depth * share, width)] * coils + [image],
        [(2, depth, slabs, step, width)],
    )(*exchange(back), residual, coil_maps, warm_start, scaled_dual)
    shares = [
        values if k == 0 else spread_over("coil", coils, k)(values)
        for k, values in enumerate(shares)
    ]
    shrunk = call(
        functools.partial(shrink_kernel, depth), "shrink", [(2 * depth * share, width)]
    )(*shares)
    shrunk = [
        shrunk if k == 0 else spread_over("coil", coils, k)(shrunk) for k in range(coils)
    ]
    return tuple(
        call(functools.partial(finish_kernel, depth), "finish", [image, (1, *image)])(
            *shrunk, summed
        )
    )


def solution(mesh):
    placed = (
        P("coil", None, "slab", None, None),
        P("coil", None, "slab", None, None),
        P(None, "slab", None, None),
        P("coil", None, None, "slab", None),
        P("coil", None, "slab", None, None),
        P(),
    )
    return jax.shard_map(
        per_device,
        mesh=mesh,
        in_specs=placed,
        out_specs=(P(None, "slab", None, None), P("coil", None, "slab", None, None)),
        check_vma=False,
    )
```

```python
import functools
import math

import jax
import jax.numpy as jnp
import numpy as np
from jax import lax
from jax.experimental import pallas as pl
from jax.experimental.pallas import tpu as pltpu
from jax.sharding import PartitionSpec as P

THRESHOLD = 0.15
ROOT_HALF = 0.7071067811865476
UNSEEN = 1e-20
F32 = jnp.float32
BF16 = jnp.bfloat16


def dft_table(length):
    index = np.arange(length)
    angles = (np.outer(index, index) % length) * (2.0 * math.pi / length)
    cosine = np.cos(angles) / math.sqrt(length)
    sine = np.sin(angles) / math.sqrt(length)
    whole = np.block([[cosine, sine], [-sine, cosine]]).astype(np.float32)
    high = whole.astype(jnp.bfloat16)
    low = (whole - high.astype(np.float32)).astype(jnp.bfloat16)
    return np.stack([high, low])


def halves(values):
    high = values.astype(BF16)
    return high, (values - high.astype(F32)).astype(BF16)


def contract(left, right, dims):
    return lax.dot_general(left, right, (dims, ((), ())), preferred_element_type=F32)


def rows_times_table(values, table_ref):
    high, low = halves(values)
    dims = ((1,), (1,))
    return (
        contract(high, table_ref[0], dims)
        + contract(high, table_ref[1], dims)
        + contract(low, table_ref[0], dims)
    )


def table_times_columns(table_ref, values):
    high, low = halves(values)
    dims = ((1,), (0,))
    return (
        contract(table_ref[0], high, dims)
        + contract(table_ref[1], high, dims)
        + contract(table_ref[0], low, dims)
    )


def fourier(real, imag, sign):
    count = len(real)
    if count == 1:
        return list(real), list(imag)
    if count % 2:
        out_real, out_imag = [], []
        for k in range(count):
            sum_real, sum_imag = real[0], imag[0]
            for n in range(1, count):
                angle = sign * 2.0 * math.pi * (k * n % count) / count
                c, s = math.cos(angle), math.sin(angle)
                sum_real = sum_real + (c * real[n] - s * imag[n])
                sum_imag = sum_imag + (c * imag[n] + s * real[n])
            out_real.append(sum_real)
            out_imag.append(sum_imag)
        return out_real, out_imag
    even_real, even_imag = fourier(real[0::2], imag[0::2], sign)
    odd_real, odd_imag = fourier(real[1::2], imag[1::2], sign)
    half = count // 2
    out_real, out_imag = [None] * count, [None] * count
    for k in range(half):
        x, y = odd_real[k], odd_imag[k]
        if k == 0:
            pass
        elif 4 * k == count:
            x, y = (-y, x) if sign > 0 else (y, -x)
        elif 8 * k == count:
            x, y = (x - sign * y) * ROOT_HALF, (y + sign * x) * ROOT_HALF
        elif 8 * k == 3 * count:
            x, y = (-x - sign * y) * ROOT_HALF, (sign * x - y) * ROOT_HALF
        else:
            angle = sign * 2.0 * math.pi * k / count
            c, s = math.cos(angle), math.sin(angle)
            x, y = c * x - s * y, c * y + s * x
        out_real[k], out_imag[k] = even_real[k] + x, even_imag[k] + y
        out_real[k + half], out_imag[k + half] = even_real[k] - x, even_imag[k] - y
    return out_real, out_imag


def total(values):
    return jnp.sum(values, axis=(0, 1), keepdims=True)


def row_tiles(count):
    step = 8 if count % 8 == 0 else count
    return [(start, step) for start in range(0, count, step)]


def placement():
    index = lax.axis_index("slab")
    return index >> 1, index & 1


def row_of(index, size):
    return pl.ds(pl.multiple_of(index * size, size), size)


def passed_on(chips, k):
    return 2 * k > chips


def routes(chips):
    far = [k for k in range(chips - 1, 0, -1) if passed_on(chips, k)]
    near = [k for k in range(1, chips) if not passed_on(chips, k)]
    return (
        [(k, 0) for k in far]
        + [(k, j) for k in near for j in range(2)]
        + [(0, 0), (0, 1)]
        + [(k, 1) for k in far[::-1]]
    )


def arrivals(chips, refs):
    chip, core = placement()
    return [
        (2 * (chip ^ k) + (core ^ j), ref) for (k, j), ref in zip(routes(chips), refs[: 2 * chips])
    ]


def departures(refs):
    chip, core = placement()
    return [
        (2 * (chip ^ k) + (core ^ j), ref.at[j]) for k, ref in enumerate(refs) for j in range(2)
    ]


def send_start_kernel(depth, given, *refs):
    sources, out_refs, held = refs[:given], refs[given : -given - 2], refs[-given - 2 : -2]
    work_ref, sems = refs[-2:]
    fetches = [
        pltpu.make_async_copy(source, target, sems.at[index])
        for index, (source, target) in enumerate(zip(sources, held))
    ]
    for fetch in fetches:
        fetch.start()
    for fetch in fetches[:2]:
        fetch.wait()
    start_ref, maps_ref, row_table, col_table = held[0], held[1], held[2], held[-1]
    _, rows, width = out_refs[0].shape
    height = start_ref.shape[3]
    step = rows // (2 * depth)
    real, imag = start_ref[0, 0], start_ref[0, 1]
    map_real, map_imag = maps_ref[0, 0], maps_ref[0, 1]
    seen_real = (map_real * real - map_imag * imag).reshape(depth * height, width)
    seen_imag = (map_real * imag + map_imag * real).reshape(depth * height, width)
    for fetch in fetches[2:]:
        fetch.wait()
    along_y = rows_times_table(jnp.concatenate([seen_real, seen_imag], axis=1), row_table)
    columns = jnp.concatenate(
        [
            jnp.concatenate(
                [
                    along_y[z * height : (z + 1) * height, part * width : (part + 1) * width]
                    for z in range(depth)
                ],
                axis=1,
            )
            for part in range(2)
        ],
        axis=0,
    )
    spectrum = table_times_columns(col_table, columns)
    for part in range(2):
        for block in range(height // step):
            first = part * height + block * step
            work_ref[part, block] = spectrum[first : first + step]
    for block, out_ref in departures(out_refs):
        for part in range(2):
            for z in range(depth):
                out_ref[pl.ds((part * depth + z) * step, step), :] = work_ref[
                    part, block, :, z * width : (z + 1) * width
                ]


def sampled_residual_kernel(depth, chips, *refs):
    kspace_ref, mask_ref = refs[2 * chips : 2 * chips + 2]
    out_refs, work_ref = refs[2 * chips + 2 : -1], refs[-1]
    length, step = kspace_ref.shape[2], kspace_ref.shape[3]
    span = depth * step
    norm = 1.0 / math.sqrt(length)
    for slab, source in arrivals(chips, refs):
        for part in range(2):
            work_ref[part, row_of(slab, span), :] = source[0, pl.ds(part * span, span), :]
    for start, size in row_tiles(step):
        rows = [pl.ds(z * step + start, size) for z in range(length)]
        real = [work_ref[0, row, :] for row in rows]
        imag = [work_ref[1, row, :] for row in rows]
        real, imag = fourier(real, imag, -1.0)
        for z in range(length):
            weight = mask_ref[pl.ds(z, 1), :].astype(F32) * norm
            real[z] = weight * (kspace_ref[0, 0, z, pl.ds(start, size), :] - norm * real[z])
            imag[z] = weight * (kspace_ref[0, 1, z, pl.ds(start, size), :] - norm * imag[z])
        real, imag = fourier(real, imag, 1.0)
        for z, row in enumerate(rows):
            work_ref[0, row, :], work_ref[1, row, :] = real[z], imag[z]
    for slab, out_ref in departures(out_refs):
        for part in range(2):
            out_ref[pl.ds(part * span, span), :] = work_ref[part, row_of(slab, span), :]


def residual_kernel(depth, chips, *refs):
    (start_ref, dual_ref, consensus_ref, maps_ref, row_table, col_table) = refs[
        2 * chips : 2 * chips + 6
    ]
    residual_ref, unseen_ref = refs[2 * chips + 6 : 2 * chips + 8]
    send_refs, (work_ref, plane_ref) = refs[2 * chips + 8 : -2], refs[-2:]
    _, rows, width = refs[0].shape
    height = start_ref.shape[3]
    step = rows // (2 * depth)
    for block, source in arrivals(chips, refs):
        for part in range(2):
            for z in range(depth):
                work_ref[part, block, :, z * width : (z + 1) * width] = source[
                    0, pl.ds((part * depth + z) * step, step), :
                ]
    blocks = height // step
    columns = jnp.concatenate(
        [work_ref[part, block] for part in (1, 0) for block in range(blocks)], axis=0
    )
    along_x = table_times_columns(col_table, columns)
    rows = jnp.concatenate(
        [
            jnp.concatenate(
                [
                    along_x[part * height : (part + 1) * height, z * width : (z + 1) * width]
                    for part in range(2)
                ],
                axis=1,
            )
            for z in range(depth)
        ],
        axis=0,
    )
    image = rows_times_table(rows, row_table)
    unseen = jnp.zeros((8, width), F32)
    for z in range(depth):
        back_imag = image[z * height : (z + 1) * height, :width]
        back_real = image[z * height : (z + 1) * height, width:]
        map_real, map_imag = maps_ref[0, 0, z], maps_ref[0, 1, z]
        pull_real = consensus_ref[0, z] - dual_ref[0, 0, z] - start_ref[0, 0, z]
        pull_imag = consensus_ref[1, z] - dual_ref[0, 1, z] - start_ref[0, 1, z]
        real = map_real * back_real + map_imag * back_imag + pull_real
        imag = map_real * back_imag - map_imag * back_real + pull_imag
        residual_ref[0, z], residual_ref[1, z] = real, imag
        power = map_real * map_real + map_imag * map_imag
        hidden = jnp.where(power < UNSEEN, real * real + imag * imag, 0.0)
        unseen = unseen + jnp.sum(hidden.reshape(height // 8, 8, width), axis=0)
        for part, plane in enumerate(
            (map_real * real - map_imag * imag, map_real * imag + map_imag * real, power)
        ):
            for block in range(blocks):
                plane_ref[part, z, block] = plane[block * step : (block + 1) * step]
    unseen_ref[...] = unseen
    for block, send_ref in departures(send_refs):
        for part in range(3):
            for z in range(depth):
                send_ref[pl.ds((part * depth + z) * step, step), :] = plane_ref[part, z, block]


def normal_kernel(depth, chips, *refs):
    unseen_ref, mask_ref, row_table = refs[2 * chips : 2 * chips + 3]
    out_refs, (seen_ref, work_ref, held_ref) = refs[2 * chips + 3 : -3], refs[-3:]
    _, rows, width = refs[0].shape
    span = rows // 3
    step = span // depth
    length = depth * chips * 2
    norm = 1.0 / math.sqrt(length)
    for slab, source in arrivals(chips, refs):
        for part in range(3):
            seen_ref[part, row_of(slab, span), :] = source[0, pl.ds(part * span, span), :]

    def place(z, start):
        return z * step + start

    def weigh(z):
        return mask_ref[pl.ds(z, 1), :].astype(F32) * norm

    seen_real, seen_imag = seen_ref[0], seen_ref[1]
    along_y = rows_times_table(jnp.concatenate([seen_real, seen_imag], axis=1), row_table)
    work_ref[0], work_ref[1] = along_y[:, :width], along_y[:, width:]
    sampled = None
    for start, size in row_tiles(step):
        real = [work_ref[0, pl.ds(place(z, start), size), :] for z in range(length)]
        imag = [work_ref[1, pl.ds(place(z, start), size), :] for z in range(length)]
        real, imag = fourier(real, imag, -1.0)
        for z in range(length):
            weight = weigh(z)
            real[z], imag[z] = real[z] * weight, imag[z] * weight
            held_ref[0, pl.ds(place(z, start), size), :] = real[z]
            held_ref[1, pl.ds(place(z, start), size), :] = imag[z]
            term = real[z] * real[z] + imag[z] * imag[z]
            sampled = term if sampled is None else sampled + term
        real, imag = fourier(real, imag, 1.0)
        for z in range(length):
            work_ref[0, pl.ds(place(z, start), size), :] = real[z] * norm
            work_ref[1, pl.ds(place(z, start), size), :] = imag[z] * norm
    image = rows_times_table(jnp.concatenate([work_ref[1], work_ref[0]], axis=1), row_table)
    back_real, back_imag = image[:, width:], image[:, :width]
    work_ref[0], work_ref[1] = back_real, back_imag
    for slab, out_ref in departures(out_refs):
        for part in range(2):
            out_ref[pl.ds(part * span, span), :] = work_ref[part, row_of(slab, span), :]
    power = seen_ref[2]
    inverse = jnp.where(power < UNSEEN, 0.0, 1.0 / jnp.maximum(power, UNSEEN))
    first = total((seen_real * seen_real + seen_imag * seen_imag) * inverse)
    sampled = total(sampled)
    slope = jnp.where(first > 0.0, sampled / jnp.where(first > 0.0, first, 1.0), 0.0)
    rest_real = power * back_real - slope * seen_real
    rest_imag = power * back_imag - slope * seen_imag
    spread = total((rest_real * rest_real + rest_imag * rest_imag) * inverse)
    along_y = rows_times_table(jnp.concatenate([rest_real, rest_imag], axis=1), row_table)
    work_ref[0], work_ref[1] = along_y[:, :width], along_y[:, width:]
    energy, cross = None, None
    for start, size in row_tiles(step):
        real = [work_ref[0, pl.ds(place(z, start), size), :] for z in range(length)]
        imag = [work_ref[1, pl.ds(place(z, start), size), :] for z in range(length)]
        real, imag = fourier(real, imag, -1.0)
        for z in range(length):
            weight = weigh(z)
            real[z], imag[z] = real[z] * weight, imag[z] * weight
            term = real[z] * real[z] + imag[z] * imag[z]
            other_term = (
                real[z] * held_ref[0, pl.ds(place(z, start), size), :]
                + imag[z] * held_ref[1, pl.ds(place(z, start), size), :]
            )
            energy = term if energy is None else energy + term
            cross = other_term if cross is None else cross + other_term
    line = lax.broadcasted_iota(jnp.int32, (8, width), 0)
    sums = jnp.zeros((8, width), F32)
    shares = (first, sampled, spread, total(energy), total(cross), total(unseen_ref[...]))
    for index, share in enumerate(shares):
        sums = jnp.where(line == index, share, sums)
    for out_ref in out_refs:
        for j in range(2):
            out_ref[j, pl.ds(2 * span, 8), :] = sums


def combine_kernel(depth, chips, *refs):
    residual_ref, maps_ref, start_ref, dual_ref = refs[2 * chips : 2 * chips + 4]
    send_refs, sum_ref, back_ref = refs[2 * chips + 4 : -2], refs[-2], refs[-1]
    _, rows, width = refs[0].shape
    span = (rows - 8) // 2
    step = span // depth
    height = start_ref.shape[3]
    parts = len(send_refs)
    share = height // parts
    sources = arrivals(chips, refs)
    sums = [source[0, pl.ds(2 * span, 8), :] for _, source in sources]
    added = functools.reduce(lambda a, b: a + b, sums)
    unseen = added[5:6]
    norm_first = added[0:1] + unseen
    sampled = added[1:2]
    slope = sampled / norm_first
    spread = slope * slope * unseen
    energy = jnp.zeros_like(unseen)
    for shares in sums:
        own, own_sampled = shares[0:1], shares[1:2]
        own_slope = jnp.where(own > 0.0, own_sampled / jnp.where(own > 0.0, own, 1.0), 0.0)
        shift = slope - own_slope
        spread = spread + shares[2:3] + shift * shift * own
        energy = energy + shares[3:4] - 2.0 * shift * shares[4:5] + shift * shift * own_sampled
    alpha_first = norm_first / (norm_first + sampled)
    beta = alpha_first * alpha_first * spread / norm_first
    curve = spread + energy - alpha_first * spread * spread / norm_first
    alpha_second = jnp.where(spread > 0.0, spread / jnp.where(spread > 0.0, curve, 1.0), 0.0)
    along_residual = alpha_first + alpha_second * (alpha_first * slope + beta)
    along_back = -alpha_first * alpha_second
    for block, source in sources:
        for part in range(2):
            for z in range(depth):
                back_ref[part, z, block] = source[0, pl.ds(part * span + z * step, step), :]
    for block in range(height // step):
        window = pl.ds(block * step, step)
        for z in range(depth):
            back_real = back_ref[0, z, block] * along_back
            back_imag = back_ref[1, z, block] * along_back
            map_real, map_imag = maps_ref[0, 0, z, window, :], maps_ref[0, 1, z, window, :]
            moves = (
                map_real * back_real + map_imag * back_imag,
                map_real * back_imag - map_imag * back_real,
            )
            for part in range(2):
                sum_ref[part, z, window, :] = (
                    start_ref[0, part, z, window, :]
                    + dual_ref[0, part, z, window, :]
                    + along_residual * residual_ref[part, z, window, :]
                    + moves[part]
                )
    coil = lax.axis_index("coil")
    for k in range(parts):
        window = row_of(coil ^ k, share)
        for part in range(2):
            for z in range(depth):
                send_refs[k][pl.ds((part * depth + z) * share, share), :] = sum_ref[
                    part, z, window, :
                ]


def shrink_kernel(depth, *refs):
    all_refs, out_ref = refs[:-1], refs[-1]
    coils = len(all_refs)
    rows, width = out_ref.shape
    share = rows // (2 * depth)
    line = lax.broadcasted_iota(jnp.int32, (share, width), 0) % 2
    lane = lax.broadcasted_iota(jnp.int32, (share, width), 1) % 2
    low = (line == 0) & (lane == 0)

    def along_lines(cells):
        near = jnp.where(
            line == 0, pltpu.roll(cells, share - 1, 0), pltpu.roll(cells, 1, 0) - 2.0 * cells
        )
        return (cells + near) * ROOT_HALF

    def along_lanes(cells):
        near = jnp.where(
            lane == 0, pltpu.roll(cells, width - 1, 1), pltpu.roll(cells, 1, 1) - 2.0 * cells
        )
        return (cells + near) * ROOT_HALF

    def mean(part, z):
        window = pl.ds((part * depth + z) * share, share)
        return functools.reduce(lambda a, b: a + b, [ref[window, :] for ref in all_refs]) * (
            1.0 / coils
        )

    for z in range(0, depth, 2):
        bands = []
        for part in range(2):
            first, second = mean(part, z), mean(part, z + 1)
            bands.append(
                [
                    along_lanes(along_lines(band))
                    for band in ((first + second) * ROOT_HALF, (first - second) * ROOT_HALF)
                ]
            )
        kept = [[], []]
        for level in range(2):
            real, imag = bands[0][level], bands[1][level]
            size = jnp.sqrt(real * real + imag * imag)
            factor = jnp.maximum(size - THRESHOLD, 0.0) / jnp.maximum(size, THRESHOLD)
            if level == 0:
                factor = jnp.where(low, 1.0, factor)
            kept[0].append(along_lines(along_lanes(real * factor)))
            kept[1].append(along_lines(along_lanes(imag * factor)))
        for part in range(2):
            base, detail = kept[part]
            out_ref[pl.ds((part * depth + z) * share, share), :] = (base + detail) * ROOT_HALF
            out_ref[pl.ds((part * depth + z + 1) * share, share), :] = (base - detail) * ROOT_HALF


def finish_kernel(depth, *refs):
    parts = len(refs) - 3
    sum_ref, consensus_ref, dual_ref = refs[parts:]
    share = refs[0].shape[0] // (2 * depth)
    coil = lax.axis_index("coil")
    for k in range(parts):
        window = row_of(coil ^ k, share)
        for part in range(2):
            for z in range(depth):
                cells = refs[parts - 1 - k][pl.ds((part * depth + z) * share, share), :]
                consensus_ref[part, z, window, :] = cells
                dual_ref[0, part, z, window, :] = sum_ref[part, z, window, :] - cells


def call(kernel, name, outs, scratch=(), fetched=False):
    in_vmem = pl.BlockSpec(memory_space=pltpu.VMEM)
    left = pl.BlockSpec(memory_space=pltpu.HBM)
    shapes = [jax.ShapeDtypeStruct(shape, F32) for shape in outs]

    def run(*operands):
        return pl.pallas_call(
            kernel,
            name=name,
            out_shape=shapes if len(shapes) > 1 else shapes[0],
            in_specs=[left if fetched else in_vmem] * len(operands),
            out_specs=[in_vmem] * len(shapes) if len(shapes) > 1 else in_vmem,
            scratch_shapes=[pltpu.VMEM(s, F32) if isinstance(s, tuple) else s for s in scratch],
            compiler_params=pltpu.CompilerParams(vmem_limit_bytes=32 << 20),
        )(*operands)

    return run


def spread_over(axis, size, mask):
    return lambda values: lax.ppermute(values, axis, [(i, i ^ mask) for i in range(size)])


def per_device(warm_start, scaled_dual, consensus, kspace, coil_maps, line_mask):
    depth, height, width = warm_start.shape[2:]
    slabs, coils = lax.axis_size("slab"), lax.axis_size("coil")
    chips = slabs // 2
    step = height // slabs
    span = depth * step
    share = height // coils
    row_table = jnp.asarray(dft_table(width))
    col_table = row_table if height == width else jnp.asarray(dft_table(height))
    tables = (row_table, col_table)
    image = (2, depth, height, width)

    def exchange(pieces):
        landed = {(0, 0): pieces[0], (0, 1): spread_over("slab", slabs, 1)(pieces[0][1:2])}
        for k in range(1, chips):
            if passed_on(chips, k):
                landed[k, 0] = spread_over("slab", slabs, 2 * k)(pieces[k])
                landed[k, 1] = spread_over("slab", slabs, 1)(landed[k, 0][1:2])
                continue
            for j in range(2):
                half, _ = lax.optimization_barrier((pieces[k][j : j + 1], landed[0, 1]))
                landed[k, j] = spread_over("slab", slabs, 2 * k + j)(half)
        return [landed[route] for route in routes(chips)]

    piece = (2, 2 * span, width)
    own_tables = tables[:1] if row_table is col_table else tables
    fetched = (warm_start, coil_maps, *own_tables)
    seen = call(
        functools.partial(send_start_kernel, depth, len(fetched)),
        "send_start",
        [piece] * chips,
        [
            warm_start.shape,
            coil_maps.shape,
            *(pltpu.VMEM(table.shape, BF16) for table in own_tables),
            (2, slabs, step, depth * width),
            pltpu.SemaphoreType.DMA((len(fetched),)),
        ],
        fetched=True,
    )(*(pltpu.with_memory_space_constraint(operand, pltpu.HBM) for operand in fetched))
    back = call(
        functools.partial(sampled_residual_kernel, depth, chips),
        "sampled_residual",
        [piece] * chips,
        [(2, slabs * span, width)],
    )(*exchange(seen), kspace, line_mask)
    residual, unseen, *seen = call(
        functools.partial(residual_kernel, depth, chips),
        "residual",
        [image, (8, width)] + [(2, 3 * span, width)] * chips,
        [(2, slabs, step, depth * width), (3, depth, slabs, step, width)],
    )(*exchange(back), warm_start, scaled_dual, consensus, coil_maps, *tables)
    back = call(
        functools.partial(normal_kernel, depth, chips),
        "normal",
        [(2, 2 * span + 8, width)] * chips,
        [(parts, slabs * span, width) for parts in (3, 2, 2)],
    )(*exchange(seen), unseen, line_mask, row_table)
    *shares, summed = call(
        functools.partial(combine_kernel, depth, chips),
        "combine",
        [(2 * depth * share, width)] * coils + [image],
        [(2, depth, slabs, step, width)],
    )(*exchange(back), residual, coil_maps, warm_start, scaled_dual)
    shares = [
        values if k == 0 else spread_over("coil", coils, k)(values)
        for k, values in enumerate(shares)
    ]
    shrunk = call(
        functools.partial(shrink_kernel, depth), "shrink", [(2 * depth * share, width)]
    )(*shares)
    shrunk = [
        shrunk if k == 0 else spread_over("coil", coils, k)(shrunk) for k in reversed(range(coils))
    ]
    return tuple(
        call(functools.partial(finish_kernel, depth), "finish", [image, (1, *image)])(
            *shrunk, summed
        )
    )


def solution(mesh):
    placed = (
        P("coil", None, "slab", None, None),
        P("coil", None, "slab", None, None),
        P(None, "slab", None, None),
        P("coil", None, None, "slab", None),
        P("coil", None, "slab", None, None),
        P(),
    )
    return jax.shard_map(
        per_device,
        mesh=mesh,
        in_specs=placed,
        out_specs=(P(None, "slab", None, None), P("coil", None, "slab", None, None)),
        check_vma=False,
    )
```
